768 devices in a mesh: tile: 12 (over z_hi, x), lev: 64 (over z_lo, y, core).
Axes of the slice: x: 4, y: 8, z: 12 (z_hi: 3, z_lo: 4; z = z_hi * 4 + z_lo), core: 2. Of those that a mesh axis runs over, the one named last changes fastest.
Arguments:
- control: float32 [64, 768, 1024], P('lev', 'tile'), may hold values from -6 to 6
- gain: float32 [64, 768, 1024], P('lev', 'tile'), may hold values from 0.25 to 1.75
- north_coef: float32 [64, 768, 1024], P('lev', 'tile'), may hold values from 0.02 to 0.24
- east_coef: float32 [64, 768, 1024], P('lev', 'tile'), may hold values from 0.02 to 0.24
- land_sea: int32 [64, 768, 1024], P('lev', 'tile'), may hold values 0 or 1
- region: int32 [768, 1024], P(('tile', 'lev')), may hold values from 0 to 15
- tiles: float32 [16, 2, 32, 32], replicated, may hold values from -0.5 to 1.5
Outputs:
- increment: float32 [64, 768, 1024], P('lev', 'tile')
The draws below stay inside these ranges and needn't reach their ends.
All inputs are finite; a program needn't handle non-finite values. No bound on the sum of `land_sea` on one device may be relied on, other than what follows from the above.
Results may differ from the reference program's by a relative error of at most 0.0003.
Values sent between devices are 32-bit elements; how exact they have to be, the bound alone decides.
A program may use at most 32 MiB of HBM per device.

```python
import math
import jax
import jax.numpy as jnp
from jax import lax

FIELDS = 2
LEVELS = 32
STEPS = 10
REGIONS = 16
NXC = 1024
SLABS = 64
NY = 768


def draw_tiles(key, part):
    shape = (REGIONS, FIELDS, LEVELS, LEVELS)
    factor = 0.6 / LEVELS ** 0.5
    spread = jnp.clip(jax.random.normal(key, shape, jnp.float32), -4.0, 4.0)
    eye_block = jnp.eye(LEVELS, dtype=jnp.float32)[None, None, :, :]
    return (eye_block + factor * spread).astype(jnp.float32)


def set_ends(values, own_key, low, largest):
    longest = values.shape.index(max(values.shape))
    spots = []
    for shift in (0, 1):
        where = [jax.random.randint(jax.random.fold_in(own_key, axis), (), 0, length) for axis, length in enumerate(values.shape)]
        where[longest] = (where[longest] + shift) % values.shape[longest]
        spots.append(tuple(where))
    return values.at[spots[0]].set(low).at[spots[1]].set(largest)


def level_of(key, extent, cuts, low, largest):
    factor_of = 1.0
    for dim, shards_of in cuts:
        draws = jax.random.uniform(jax.random.fold_in(jax.random.fold_in(key, 6), dim), (shards_of,), jnp.float32, low / len(cuts), largest / len(cuts))
        factor_of = factor_of * jnp.repeat(jnp.exp(draws), extent[dim] // shards_of).reshape((-1,) + (1,) * (len(extent) - 1 - dim))
    return factor_of


def scatter_about(rng, dims, scale, most, cuts=(), kind=jnp.bfloat16):
    values = scale * jax.random.normal(rng, dims, jnp.float32)
    if cuts:
        values = values * level_of(rng, dims, cuts, -0.22, 0.18)
    return jnp.clip(values, -most, most).astype(kind)


def setup_inputs(seed: int = 0) -> dict:
    seeds = jax.random.split(jax.random.key(seed), 8)
    return {
        "control": scatter_about(seeds[0], (SLABS, NY, NXC), 1.0, 6.0, ((0, 64), (1, 12)), jnp.float32),
        "gain": jnp.clip(1.0 + 0.15 * jax.random.normal(seeds[1], (SLABS, NY, NXC), jnp.float32), 0.25, 1.75),
        "north_coef": jnp.clip(jnp.exp(math.log(0.24) - 2.4849066 * jax.random.uniform(seeds[2], (SLABS, NY, NXC), jnp.float32) ** level_of(seeds[2], (SLABS, NY, NXC), ((0, 64), (1, 12)), -0.2, 0.2)), 0.02, 0.24),
        "east_coef": jnp.clip(jnp.exp(math.log(0.24) - 2.4849066 * jax.random.uniform(seeds[3], (SLABS, NY, NXC), jnp.float32) ** level_of(seeds[3], (SLABS, NY, NXC), ((0, 64), (1, 12)), -0.2, 0.2)), 0.02, 0.24),
        "land_sea": set_ends((jax.random.randint(seeds[4], (SLABS, NY, NXC), 0, 5) < 4).astype(jnp.int32), jax.random.fold_in(seeds[4], 1), 0, 1),
        "region": set_ends(jax.random.randint(seeds[5], (NY, NXC), 0, REGIONS), jax.random.fold_in(seeds[5], 1), 0, REGIONS - 1).astype(jnp.int32),
        "tiles": draw_tiles(jax.random.fold_in(seeds[7], 71), 0),
    }


def diffusion_step(field, north_face, east_face, ocean):
    centre = field[:, 1:-1]
    north = north_face[:, 1:-1] * (field[:, 2:] - centre)
    south = north_face[:, :-2] * (centre - field[:, :-2])
    border = jnp.zeros_like(centre[:, :, :1])
    eastward = jnp.concatenate([centre[:, :, 1:], border], axis=2)
    east_flux = east_face[:, 1:-1] * (eastward - centre)
    west_flux = jnp.concatenate([border, east_flux[:, :, :-1]], axis=2)
    return ocean[:, 1:-1] * (centre + north - south + east_flux - west_flux)


def pad_rows(array):
    return jnp.pad(array, ((0, 0), (1, 1), (0, 0)))


def diffuse(field, north_coef, east_coef, ocean):
    north_pad = pad_rows(north_coef)
    east_pad = pad_rows(east_coef)
    ocean_pad = pad_rows(ocean)
    for repeat in range(STEPS):
        field = diffusion_step(pad_rows(field), north_pad, east_pad, ocean_pad)
    return field


def regional_apply(matrices, column, flat_region):
    def accumulate(total, which):
        product = jnp.einsum("fij,fjc->fic", matrices[which], column, precision=lax.Precision.HIGHEST)
        chosen = (flat_region == which)[None, None, :]
        return total + jnp.where(chosen, product, jnp.float32(0.0)), None

    start = jnp.zeros(column.shape, jnp.float32)
    result, unused = lax.scan(accumulate, start, jnp.arange(REGIONS, dtype=jnp.int32))
    return result


def reference(control, gain, north_coef, east_coef, land_sea, region, tiles):
    ocean = land_sea.astype(jnp.float32)
    forward = diffuse(ocean * gain * control, north_coef, east_coef, ocean)
    column = forward.reshape(FIELDS, LEVELS, NY * NXC)
    flat_region = region.reshape(-1)
    column_out = regional_apply(tiles, column, flat_region)
    mixed = regional_apply(jnp.swapaxes(tiles, 2, 3), column_out, flat_region)
    mixed = mixed.reshape(SLABS, NY, NXC)
    return gain * diffuse(ocean * mixed, north_coef, east_coef, ocean)
```

```python
import functools

import jax
import jax.numpy as jnp
from jax import lax
from jax.experimental import pallas as pl
from jax.experimental.pallas import tpu as pltpu
from jax.sharding import PartitionSpec as P

FIELDS = 2
LEVELS = 32
STEPS = 10
REGIONS = 16
ROWS = 64
COLS = 1024
SUB = 8
LANE = 128
HALO = 10
HIGH = HALO + ROWS
ALL = HALO + ROWS + HALO
FIRST = (10,)
SECOND = (10,)
BLOCK = 14
MESH = pl.DeviceIdType.MESH
F32 = jnp.float32
BF16 = jnp.bfloat16


def rows_of(ref, start, count):
    return ref[pl.ds(SUB * start, SUB * count), :].reshape(count, SUB, LANE)


def put_rows(ref, start, value):
    count = value.shape[0]
    ref[pl.ds(SUB * start, SUB * count), :] = value.reshape(count * SUB, LANE)


def east_of(x, lane):
    near = pltpu.roll(x, LANE - 1, 2)
    return jnp.where(lane == LANE - 1, pltpu.roll(near, SUB - 1, 1), near)


def west_of(x, lane):
    near = pltpu.roll(x, 1, 2)
    return jnp.where(lane == 0, pltpu.roll(near, 1, 1), near)


def kernel(
    control_hbm, gain_hbm, north_hbm, east_hbm, land_hbm, region_hbm, tiles_hbm,
    out_ref,
    control, gain, north, east, land, region, tiles,
    base, ua, ub, ca, cn, cs, ce, cw,
    low_past, high_past, sent, got, gathered, column, mixed, returned,
    product, weights,
    in_sem, halo_send, halo_recv, late_send, late_recv, stage_send, stage_recv, region_sem, all_sem,
):
    tile = lax.axis_index("tile")
    lev = lax.axis_index("lev")
    tile_count = lax.axis_size("tile")
    which = lev // LEVELS
    mine = lax.rem(lev, LEVELS)
    last = tile_count - 1

    loads = [
        pltpu.make_async_copy(land_hbm.at[0], land, in_sem.at[0]),
        pltpu.make_async_copy(north_hbm.at[0], north, in_sem.at[1]),
        pltpu.make_async_copy(east_hbm.at[0], east, in_sem.at[2]),
        pltpu.make_async_copy(gain_hbm.at[0], gain, in_sem.at[3]),
        pltpu.make_async_copy(control_hbm.at[0], control, in_sem.at[4]),
        pltpu.make_async_copy(region_hbm, region.at[which], in_sem.at[5]),
        pltpu.make_async_copy(tiles_hbm.at[:, which], tiles, in_sem.at[6]),
    ]
    for load in loads:
        load.start()

    barrier = pltpu.get_barrier_semaphore()

    def group_peer(shift):
        return which * LEVELS + lax.rem(mine + shift, LEVELS)

    @pl.when(tile > 0)
    def _():
        pl.semaphore_signal(barrier, inc=1, device_id={"tile": tile - 1}, device_id_type=MESH)

    @pl.when(tile < last)
    def _():
        pl.semaphore_signal(barrier, inc=1, device_id={"tile": tile + 1}, device_id_type=MESH)

    partner = lax.rem(lev + LEVELS, FIELDS * LEVELS)
    pl.semaphore_signal(barrier, inc=1, device_id={"lev": partner}, device_id_type=MESH)

    def greet(shift, carry):
        pl.semaphore_signal(barrier, inc=1, device_id={"lev": group_peer(shift)}, device_id_type=MESH)
        return carry

    lax.fori_loop(1, LEVELS, greet, 0)

    for load in loads[:5]:
        load.wait()

    def relayout(block, carry):
        r = pl.multiple_of(block * SUB, SUB)
        for c in range(SUB):
            at = (pl.ds(r, SUB), slice(c * LANE, (c + 1) * LANE))
            to = pl.ds((HALO + r) * SUB + c, SUB, stride=SUB)
            ocean = land[at].astype(F32)
            base[0, to, :] = north[at]
            base[1, to, :] = east[at]
            base[2, to, :] = ocean
            start = ocean * gain[at] * control[at]
            base[3, to, :] = start
            ua[to, :] = start
        return carry

    lax.fori_loop(0, ROWS // SUB, relayout, 0)
    loads[5].wait()

    pl.semaphore_wait(barrier, LEVELS + jnp.minimum(tile, 1) + jnp.minimum(last - tile, 1))

    def rim(arrays, start, count):
        return base.at[pl.ds(0, arrays), pl.ds(SUB * start, SUB * count), :]

    def rims(arrays, near, count, send_sem, recv_sem):
        lower = pltpu.make_async_remote_copy(
            src_ref=rim(arrays, HALO + near, count), dst_ref=rim(arrays, HIGH + near, count),
            send_sem=send_sem.at[0], recv_sem=recv_sem.at[0],
            device_id={"tile": tile - 1}, device_id_type=MESH,
        )
        upper = pltpu.make_async_remote_copy(
            src_ref=rim(arrays, HIGH - near - count, count), dst_ref=rim(arrays, HALO - near - count, count),
            send_sem=send_sem.at[1], recv_sem=recv_sem.at[1],
            device_id={"tile": tile + 1}, device_id_type=MESH,
        )
        return lower, upper

    def start_both(pair):
        pl.when(tile > 0)(pair[0].start)
        pl.when(tile < last)(pair[1].start)

    def wait_both_recv(pair):
        pl.when(tile < last)(pair[0].wait_recv)
        pl.when(tile > 0)(pair[1].wait_recv)

    def wait_both_send(pair):
        pl.when(tile > 0)(pair[0].wait_send)
        pl.when(tile < last)(pair[1].wait_send)

    near = FIRST[0]
    urgent = rims(4, 0, near, halo_send, halo_recv)
    late = rims(3, near, HALO - near, late_send, late_recv) if near < HALO else None
    start_both(urgent)
    region_copy = pltpu.make_async_remote_copy(
        src_ref=region.at[which], dst_ref=region.at[which],
        send_sem=region_sem.at[0], recv_sem=region_sem.at[1],
        device_id={"lev": partner}, device_id_type=MESH,
    )
    region_copy.start()

    @pl.when(tile == 0)
    def _():
        for a in range(4):
            base[a, : SUB * HALO, :] = jnp.zeros((SUB * HALO, LANE), F32)
        for g in got:
            g[0] = jnp.zeros(g.shape[1:], F32)

    @pl.when(tile == last)
    def _():
        for a in range(4):
            base[a, SUB * HIGH :, :] = jnp.zeros((SUB * HALO, LANE), F32)
        for g in got:
            g[1] = jnp.zeros(g.shape[1:], F32)

    loads[6].wait()

    def square(r, carry):
        t = tiles[r]
        m = lax.dot_general(
            t, t, (((0,), (0,)), ((), ())), precision=lax.Precision.HIGHEST, preferred_element_type=F32
        )
        product[pl.ds(pl.multiple_of(r * LEVELS, LEVELS), LEVELS), :] = m
        return carry

    lax.fori_loop(0, REGIONS, square, 0)

    def thirds(x):
        one = x.astype(BF16)
        rest = x - one.astype(F32)
        two = rest.astype(BF16)
        three = (rest - two.astype(F32)).astype(BF16)
        return one, two, three

    k_of = lax.broadcasted_iota(jnp.int32, (LEVELS, 6 * LEVELS), 0)
    j_of = lax.broadcasted_iota(jnp.int32, (LEVELS, 6 * LEVELS), 1)
    total = None
    for part, groups in zip(thirds(product[...]), ((0, 1, 3), (2, 4), (5,))):
        pick = jnp.zeros((LEVELS, 6 * LEVELS), F32)
        for g in groups:
            pick = pick + jnp.where(j_of == k_of + g * LEVELS, 1.0, 0.0)
        spread = jnp.dot(part, pick.astype(BF16), preferred_element_type=F32)
        total = spread if total is None else total + spread
    weights[...] = total.astype(BF16)

    first_lane = (1, SUB, LANE)
    lane1 = lax.broadcasted_iota(jnp.int32, first_lane, 2)
    sub1 = lax.broadcasted_iota(jnp.int32, first_lane, 1)
    west_edge = jnp.logical_and(lane1 == 0, sub1 == 0)
    east_edge = jnp.logical_and(lane1 == LANE - 1, sub1 == SUB - 1)

    def make_coef(start, count):
        shape = (count, SUB, LANE)
        lane = jnp.broadcast_to(lane1, shape)
        n = rows_of(base.at[0], start, count)
        s = rows_of(base.at[0], start - 1, count)
        e = rows_of(base.at[1], start, count)
        o = rows_of(base.at[2], start, count)
        w = jnp.where(west_edge, 0.0, west_of(e, lane))
        put_rows(ca, start, o * (1.0 - n - s - e - w))
        put_rows(cn, start, o * n)
        put_rows(cs, start, o * s)
        put_rows(ce, start, o * jnp.where(east_edge, 0.0, e))
        put_rows(cw, start, o * w)

    def coefs(start, end):
        for at in range(start, end, BLOCK):
            make_coef(at, min(BLOCK, end - at))

    def coef_block(b, carry):
        make_coef(HALO + 1 + b * 9, 9)
        return carry

    lax.fori_loop(0, (ROWS - 1) // 9, coef_block, 0)

    def advance(wide, start, count):
        lane = jnp.broadcast_to(lane1, (count, SUB, LANE))
        u = wide[1:-1]
        v = rows_of(ca, start, count) * u
        v = v + rows_of(cn, start, count) * wide[2:]
        v = v + rows_of(cs, start, count) * wide[:-2]
        v = v + rows_of(ce, start, count) * east_of(u, lane)
        return v + rows_of(cw, start, count) * west_of(u, lane)

    def inner_step(src, dst, s):
        low_past[s] = src[pl.ds(SUB * (HALO + s), 2 * SUB), :]
        high_past[s] = src[pl.ds(SUB * (HIGH - 2 - s), 2 * SUB), :]
        at, end = HALO + 1, HIGH - 1
        while at < end:
            count = min(BLOCK, end - at)
            put_rows(dst, at, advance(rows_of(src, at - 1, count + 2), at, count))
            at += count

    def inner(src, other, depth):
        def pair(i, carry):
            inner_step(src, other, 2 * i)
            inner_step(other, src, 2 * i + 1)
            return carry

        if depth // 2:
            lax.fori_loop(0, depth // 2, pair, 0)
        if depth % 2:
            inner_step(src, other, depth - 1)
            return other, src
        return src, other

    def outer(dst, low, high, depth):
        def one(s, carry):
            low, high = carry
            past = low_past[s].reshape(2, SUB, LANE)
            low = advance(jnp.concatenate([low, past], axis=0), HALO - depth + 1 + s, depth)
            past = high_past[s].reshape(2, SUB, LANE)
            high = advance(jnp.concatenate([past, high], axis=0), HIGH - 1 - s, depth)
            return low, high

        low, high = lax.fori_loop(0, depth, one, (low, high))
        put_rows(dst, HALO, low)
        put_rows(dst, HIGH - depth, high)

    def swap(field, depth, number):
        sent[number][0] = field[SUB * HALO : SUB * (HALO + depth), :]
        sent[number][1] = field[SUB * (HIGH - depth) : SUB * HIGH, :]
        lower = pltpu.make_async_remote_copy(
            src_ref=sent[number].at[0], dst_ref=got[number].at[1],
            send_sem=stage_send.at[number, 0], recv_sem=stage_recv.at[number, 0],
            device_id={"tile": tile - 1}, device_id_type=MESH,
        )
        upper = pltpu.make_async_remote_copy(
            src_ref=sent[number].at[1], dst_ref=got[number].at[0],
            send_sem=stage_send.at[number, 1], recv_sem=stage_recv.at[number, 1],
            device_id={"tile": tile + 1}, device_id_type=MESH,
        )
        start_both((lower, upper))
        return lower, upper

    swaps = []
    field, other = ua, ub
    for stage, depth in enumerate(FIRST):
        if stage:
            swaps.append(swap(field, depth, len(swaps)))
            if stage == 1:
                start_both(late)
        field, other = inner(field, other, depth)
        if stage:
            wait_both_recv(swaps[-1])
            low, high = (g.reshape(depth, SUB, LANE) for g in (got[len(swaps) - 1][0], got[len(swaps) - 1][1]))
        else:
            wait_both_recv(urgent)
            coefs(HALO - near + 1, HALO + 1)
            coefs(HIGH, HIGH + near - 1)
            low = rows_of(base.at[3], HALO - depth, depth)
            high = rows_of(base.at[3], HIGH, depth)
        outer(field, low, high, depth)

    for h in range(2):
        gathered[h] = rows_of(field, HALO + h * LEVELS, LEVELS)

    def to_columns(shift, carry):
        peer = lax.rem(mine + shift, LEVELS)
        pltpu.make_async_remote_copy(
            src_ref=gathered.at[:, peer], dst_ref=column.at[:, mine],
            send_sem=all_sem.at[0], recv_sem=all_sem.at[1],
            device_id={"lev": which * LEVELS + peer}, device_id_type=MESH,
        ).start()
        return carry

    pltpu.make_async_copy(gathered.at[:, mine], column.at[:, mine], all_sem.at[1]).start()
    lax.fori_loop(1, LEVELS, to_columns, 0)

    def wait_all(ref, sem):
        pltpu.make_async_copy(ref, ref, sem).wait()

    region_copy.wait()
    wait_all(column, all_sem.at[1])

    wide = 2 * LANE
    column2 = column.reshape(2 * LEVELS * SUB, LANE)
    mixed2 = mixed.reshape(2 * LEVELS * SUB, LANE)

    def mix(i, carry):
        h = i // (SUB // 2)
        c = 2 * lax.rem(i, SUB // 2)
        start = h * LEVELS * SUB + c
        x = jnp.concatenate(
            [column2[pl.ds(start + q, LEVELS, stride=SUB), :] for q in range(2)], axis=1
        )
        one, two, three = thirds(x)
        stacked = jnp.concatenate([one, two, one, three, two, one], axis=0)
        every = jnp.dot(weights[...], stacked, preferred_element_type=F32)
        ids = region[h, :, pl.ds(pl.multiple_of(c * LANE, wide), wide)]
        ids = jnp.broadcast_to(ids, (LEVELS, wide))
        y = every[:LEVELS]
        for r in range(1, REGIONS):
            y = jnp.where(ids == r, every[r * LEVELS : (r + 1) * LEVELS], y)
        for q in range(2):
            mixed2[pl.ds(start + q, LEVELS, stride=SUB), :] = y[:, q * LANE : (q + 1) * LANE]
        return carry

    lax.fori_loop(0, SUB, mix, 0)

    def to_levels(shift, carry):
        peer = lax.rem(mine + shift, LEVELS)
        pltpu.make_async_remote_copy(
            src_ref=mixed.at[:, peer], dst_ref=returned.at[:, mine],
            send_sem=all_sem.at[2], recv_sem=all_sem.at[3],
            device_id={"lev": which * LEVELS + peer}, device_id_type=MESH,
        ).start()
        return carry

    pltpu.make_async_copy(mixed.at[:, mine], returned.at[:, mine], all_sem.at[3]).start()
    lax.fori_loop(1, LEVELS, to_levels, 0)
    wait_all(returned, all_sem.at[3])

    field, other = ua, ub
    for h in range(2):
        o = rows_of(base.at[2], HALO + h * LEVELS, LEVELS)
        put_rows(field, HALO + h * LEVELS, o * returned[h])

    for stage, depth in enumerate(SECOND):
        swaps.append(swap(field, depth, len(swaps)))
        field, other = inner(field, other, depth)
        if stage == 0 and late is not None:
            wait_both_recv(late)
            coefs(1, HALO - near + 1)
            coefs(HIGH + near - 1, ALL - 1)
        wait_both_recv(swaps[-1])
        low, high = (g.reshape(depth, SUB, LANE) for g in (got[len(swaps) - 1][0], got[len(swaps) - 1][1]))
        outer(field, low, high, depth)

    def finish(block, carry):
        r = pl.multiple_of(block * SUB, SUB)
        for c in range(SUB):
            at = (pl.ds(r, SUB), slice(c * LANE, (c + 1) * LANE))
            out_ref[at] = gain[at] * field[pl.ds((HALO + r) * SUB + c, SUB, stride=SUB), :]
        return carry

    lax.fori_loop(0, ROWS // SUB, finish, 0)

    def sends(ref, sem):
        part = ref.at[:, pl.ds(0, LEVELS - 1)]
        pltpu.make_async_copy(part, part, sem).wait()

    sends(gathered, all_sem.at[0])
    sends(mixed, all_sem.at[2])
    wait_both_send(urgent)
    if late is not None:
        wait_both_send(late)
    for pair in swaps:
        wait_both_send(pair)


def body(*args):
    raw = pltpu.VMEM((ROWS, COLS), F32)
    field = pltpu.VMEM((ALL * SUB, LANE), F32)
    depths = FIRST[1:] + SECOND
    slots = [pltpu.VMEM((2, d * SUB, LANE), F32) for d in depths]
    cube = pltpu.VMEM((2, LEVELS, SUB, LANE), F32)
    out = pl.pallas_call(
        kernel,
        out_shape=jax.ShapeDtypeStruct((ROWS, COLS), F32),
        in_specs=[pl.BlockSpec(memory_space=pltpu.HBM)] * 7,
        out_specs=pl.BlockSpec(memory_space=pltpu.VMEM),
        scratch_shapes=[
            raw, raw, raw, raw,
            pltpu.VMEM((ROWS, COLS), jnp.int32),
            pltpu.VMEM((2, 1, COLS), jnp.int32),
            pltpu.VMEM((REGIONS, LEVELS, LEVELS), F32),
            pltpu.VMEM((4, ALL * SUB, LANE), F32),
            field, field, field, field, field, field, field,
            pltpu.VMEM((HALO, 2 * SUB, LANE), F32),
            pltpu.VMEM((HALO, 2 * SUB, LANE), F32),
            slots, slots,
            cube, cube, cube, cube,
            pltpu.VMEM((REGIONS * LEVELS, LEVELS), F32),
            pltpu.VMEM((REGIONS * LEVELS, 6 * LEVELS), BF16),
            pltpu.SemaphoreType.DMA((7,)),
            pltpu.SemaphoreType.DMA((2,)),
            pltpu.SemaphoreType.DMA((2,)),
            pltpu.SemaphoreType.DMA((2,)),
            pltpu.SemaphoreType.DMA((2,)),
            pltpu.SemaphoreType.DMA((len(depths), 2)),
            pltpu.SemaphoreType.DMA((len(depths), 2)),
            pltpu.SemaphoreType.DMA((2,)),
            pltpu.SemaphoreType.DMA((4,)),
        ],
        compiler_params=pltpu.CompilerParams(
            collective_id=0, has_side_effects=True, vmem_limit_bytes=32 * 1024 * 1024
        ),
        name="covariance",
    )(*[pltpu.with_memory_space_constraint(x, pltpu.HBM) for x in args])
    return out[None]


def solution(mesh):
    return jax.shard_map(
        body,
        mesh=mesh,
        in_specs=(
            P("lev", "tile", None),
            P("lev", "tile", None),
            P("lev", "tile", None),
            P("lev", "tile", None),
            P("lev", "tile", None),
            P(("tile", "lev"), None),
            P(),
        ),
        out_specs=P("lev", "tile", None),
        check_vma=False,
    )
```

```python
import functools

import jax
import jax.numpy as jnp
from jax import lax
from jax.experimental import pallas as pl
from jax.experimental.pallas import tpu as pltpu
from jax.sharding import PartitionSpec as P

FIELDS = 2
LEVELS = 32
STEPS = 10
REGIONS = 16
ROWS = 64
COLS = 1024
SUB = 8
LANE = 128
HALO = 10
HIGH = HALO + ROWS
ALL = HALO + ROWS + HALO
WIDE = 4
BLOCK = 14
MESH = pl.DeviceIdType.MESH
F32 = jnp.float32
BF16 = jnp.bfloat16


def rows_of(ref, start, count):
    return ref[pl.ds(SUB * start, SUB * count), :].reshape(count, SUB, LANE)


def put_rows(ref, start, value):
    count = value.shape[0]
    ref[pl.ds(SUB * start, SUB * count), :] = value.reshape(count * SUB, LANE)


def east_of(x, lane):
    near = pltpu.roll(x, LANE - 1, 2)
    return jnp.where(lane == LANE - 1, pltpu.roll(near, SUB - 1, 1), near)


def west_of(x, lane):
    near = pltpu.roll(x, 1, 2)
    return jnp.where(lane == 0, pltpu.roll(near, 1, 1), near)


def kernel(
    control_hbm, gain_hbm, north_hbm, east_hbm, land_hbm, region_hbm, tiles_hbm,
    out_ref,
    control, gain, north, east, land, region, tiles,
    base, ua, ub, ca, cn, cs, ce, cw,
    low_past, high_past, carried, sent, got, gathered, column, mixed, returned,
    product, weights,
    in_sem, halo_send, halo_recv, carry_recv, carry_send, swap_send, swap_recv, region_sem, all_sem,
):
    tile = lax.axis_index("tile")
    lev = lax.axis_index("lev")
    tile_count = lax.axis_size("tile")
    which = lev // LEVELS
    mine = lax.rem(lev, LEVELS)
    last = tile_count - 1
    place = lax.rem(tile, WIDE)
    band = tile // WIDE
    bands = tile_count // WIDE
    upper_end = jnp.logical_and(place == WIDE - 1, band < bands - 1)
    lower_end = jnp.logical_and(place == 0, band > 0)
    down_carrier = jnp.logical_and(place > 0, band > 0)
    up_carrier = jnp.logical_and(place < WIDE - 1, band < bands - 1)

    loads = [
        pltpu.make_async_copy(land_hbm.at[0], land, in_sem.at[0]),
        pltpu.make_async_copy(north_hbm.at[0], north, in_sem.at[1]),
        pltpu.make_async_copy(east_hbm.at[0], east, in_sem.at[2]),
        pltpu.make_async_copy(gain_hbm.at[0], gain, in_sem.at[3]),
        pltpu.make_async_copy(control_hbm.at[0], control, in_sem.at[4]),
        pltpu.make_async_copy(region_hbm, region.at[which], in_sem.at[5]),
        pltpu.make_async_copy(tiles_hbm.at[:, which], tiles, in_sem.at[6]),
    ]
    for load in loads:
        load.start()

    barrier = pltpu.get_barrier_semaphore()

    def group_peer(shift):
        return which * LEVELS + lax.rem(mine + shift, LEVELS)

    @pl.when(tile > 0)
    def _():
        pl.semaphore_signal(barrier, inc=1, device_id={"tile": tile - 1}, device_id_type=MESH)

    @pl.when(tile < last)
    def _():
        pl.semaphore_signal(barrier, inc=1, device_id={"tile": tile + 1}, device_id_type=MESH)

    for far in range(1, WIDE):
        for end, offset in ((upper_end, far + 1), (lower_end, far), (lower_end, -far - 1), (upper_end, -far)):
            @pl.when(end)
            def _(offset=offset):
                pl.semaphore_signal(barrier, inc=1, device_id={"tile": tile + offset}, device_id_type=MESH)

    for carrier, offset in (
        (down_carrier, -place - 1), (down_carrier, -place),
        (up_carrier, WIDE - place), (up_carrier, WIDE - 1 - place),
    ):
        @pl.when(carrier)
        def _(offset=offset):
            pl.semaphore_signal(barrier, inc=1, device_id={"tile": tile + offset}, device_id_type=MESH)

    partner = lax.rem(lev + LEVELS, FIELDS * LEVELS)
    pl.semaphore_signal(barrier, inc=1, device_id={"lev": partner}, device_id_type=MESH)

    def greet(shift, carry):
        pl.semaphore_signal(barrier, inc=1, device_id={"lev": group_peer(shift)}, device_id_type=MESH)
        return carry

    lax.fori_loop(1, LEVELS, greet, 0)

    for load in loads[:5]:
        load.wait()

    def relayout(block, carry):
        r = pl.multiple_of(block * SUB, SUB)
        for c in range(SUB):
            at = (pl.ds(r, SUB), slice(c * LANE, (c + 1) * LANE))
            to = pl.ds((HALO + r) * SUB + c, SUB, stride=SUB)
            ocean = land[at].astype(F32)
            base[0, to, :] = north[at]
            base[1, to, :] = east[at]
            base[2, to, :] = ocean
            start = ocean * gain[at] * control[at]
            base[3, to, :] = start
            ua[to, :] = start
        return carry

    lax.fori_loop(0, ROWS // SUB, relayout, 0)
    loads[5].wait()

    def as_count(flag):
        return flag.astype(jnp.int32)

    greeted = LEVELS + as_count(tile > 0) + as_count(tile < last)
    greeted = greeted + 2 * (WIDE - 1) * (as_count(upper_end) + as_count(lower_end))
    greeted = greeted + 2 * (as_count(up_carrier) + as_count(down_carrier))
    pl.semaphore_wait(barrier, greeted)

    def rim(a, start):
        return base.at[a, pl.ds(SUB * start, SUB * HALO), :]

    def send_rim(a, side, offset, to=None):
        start, land_at = ((HALO, HIGH), (HIGH - HALO, 0))[side]
        return pltpu.make_async_remote_copy(
            src_ref=rim(a, start), dst_ref=rim(a, land_at) if to is None else to,
            send_sem=halo_send.at[side, a],
            recv_sem=halo_recv.at[side, a] if to is None else carry_recv.at[side],
            device_id={"tile": tile + offset}, device_id_type=MESH,
        )

    def forward(side):
        a = (place - 1, WIDE - 2 - place)[side]
        return pltpu.make_async_remote_copy(
            src_ref=carried.at[side], dst_ref=rim(a, (HIGH, 0)[side]),
            send_sem=carry_send.at[side], recv_sem=halo_recv.at[side, a],
            device_id={"tile": tile + (-place - 1, WIDE - place)[side]}, device_id_type=MESH,
        )

    has_lower, has_upper = tile > 0, tile < last

    def start_both(pair):
        pl.when(has_lower)(pair[0].start)
        pl.when(has_upper)(pair[1].start)

    def wait_both_recv(pair):
        pl.when(has_upper)(pair[0].wait_recv)
        pl.when(has_lower)(pair[1].wait_recv)

    def wait_both_send(pair):
        pl.when(has_lower)(pair[0].wait_send)
        pl.when(has_upper)(pair[1].wait_send)

    straight = [(send_rim(a, 0, -1), send_rim(a, 1, 1)) for a in range(4)]
    for a in range(WIDE - 1):
        pl.when(lower_end)(send_rim(a, 0, 1 + a, carried.at[0]).start)
        pl.when(upper_end)(send_rim(a, 1, -1 - a, carried.at[1]).start)
        pl.when(jnp.logical_and(has_lower, jnp.logical_not(lower_end)))(straight[a][0].start)
        pl.when(jnp.logical_and(has_upper, jnp.logical_not(upper_end)))(straight[a][1].start)
    start_both(straight[3])

    def carry_on():
        for side, carrier in enumerate((down_carrier, up_carrier)):
            @pl.when(carrier)
            def _(side=side):
                copy = forward(side)
                pltpu.make_async_copy(carried.at[side], carried.at[side], carry_recv.at[side]).wait()
                copy.start()

    region_copy = pltpu.make_async_remote_copy(
        src_ref=region.at[which], dst_ref=region.at[which],
        send_sem=region_sem.at[0], recv_sem=region_sem.at[1],
        device_id={"lev": partner}, device_id_type=MESH,
    )
    region_copy.start()

    @pl.when(tile == 0)
    def _():
        for a in range(4):
            base[a, : SUB * HALO, :] = jnp.zeros((SUB * HALO, LANE), F32)
        got[0] = jnp.zeros(got.shape[1:], F32)

    @pl.when(tile == last)
    def _():
        for a in range(4):
            base[a, SUB * HIGH :, :] = jnp.zeros((SUB * HALO, LANE), F32)
        got[1] = jnp.zeros(got.shape[1:], F32)

    loads[6].wait()

    def square(r, carry):
        t = tiles[r]
        m = lax.dot_general(
            t, t, (((0,), (0,)), ((), ())), precision=lax.Precision.HIGHEST, preferred_element_type=F32
        )
        product[pl.ds(pl.multiple_of(r * LEVELS, LEVELS), LEVELS), :] = m
        return carry

    lax.fori_loop(0, REGIONS, square, 0)

    def thirds(x):
        one = x.astype(BF16)
        rest = x - one.astype(F32)
        two = rest.astype(BF16)
        three = (rest - two.astype(F32)).astype(BF16)
        return one, two, three

    k_of = lax.broadcasted_iota(jnp.int32, (LEVELS, 6 * LEVELS), 0)
    j_of = lax.broadcasted_iota(jnp.int32, (LEVELS, 6 * LEVELS), 1)
    total = None
    for part, groups in zip(thirds(product[...]), ((0, 1, 3), (2, 4), (5,))):
        pick = jnp.zeros((LEVELS, 6 * LEVELS), F32)
        for g in groups:
            pick = pick + jnp.where(j_of == k_of + g * LEVELS, 1.0, 0.0)
        spread = jnp.dot(part, pick.astype(BF16), preferred_element_type=F32)
        total = spread if total is None else total + spread
    weights[...] = total.astype(BF16)

    first_lane = (1, SUB, LANE)
    lane1 = lax.broadcasted_iota(jnp.int32, first_lane, 2)
    sub1 = lax.broadcasted_iota(jnp.int32, first_lane, 1)
    west_edge = jnp.logical_and(lane1 == 0, sub1 == 0)
    east_edge = jnp.logical_and(lane1 == LANE - 1, sub1 == SUB - 1)

    def make_coef(start, count):
        shape = (count, SUB, LANE)
        lane = jnp.broadcast_to(lane1, shape)
        n = rows_of(base.at[0], start, count)
        s = rows_of(base.at[0], start - 1, count)
        e = rows_of(base.at[1], start, count)
        o = rows_of(base.at[2], start, count)
        w = jnp.where(west_edge, 0.0, west_of(e, lane))
        put_rows(ca, start, o * (1.0 - n - s - e - w))
        put_rows(cn, start, o * n)
        put_rows(cs, start, o * s)
        put_rows(ce, start, o * jnp.where(east_edge, 0.0, e))
        put_rows(cw, start, o * w)

    def coefs(start, end):
        for at in range(start, end, BLOCK):
            make_coef(at, min(BLOCK, end - at))

    def coef_block(b, carry):
        make_coef(HALO + 1 + b * 9, 9)
        return carry

    lax.fori_loop(0, (ROWS - 1) // 9, coef_block, 0)

    def advance(wide, start, count):
        lane = jnp.broadcast_to(lane1, (count, SUB, LANE))
        u = wide[1:-1]
        v = rows_of(ca, start, count) * u
        v = v + rows_of(cn, start, count) * wide[2:]
        v = v + rows_of(cs, start, count) * wide[:-2]
        v = v + rows_of(ce, start, count) * east_of(u, lane)
        return v + rows_of(cw, start, count) * west_of(u, lane)

    def inner_step(src, dst, s):
        low_past[s] = src[pl.ds(SUB * (HALO + s), 2 * SUB), :]
        high_past[s] = src[pl.ds(SUB * (HIGH - 2 - s), 2 * SUB), :]
        at, end = HALO + 1, HIGH - 1
        while at < end:
            count = min(BLOCK, end - at)
            put_rows(dst, at, advance(rows_of(src, at - 1, count + 2), at, count))
            at += count

    def inner():
        def pair(i, carry):
            inner_step(ua, ub, 2 * i)
            inner_step(ub, ua, 2 * i + 1)
            return carry

        lax.fori_loop(0, STEPS // 2, pair, 0)

    def outer(low, high):
        def one(s, carry):
            low, high = carry
            past = low_past[s].reshape(2, SUB, LANE)
            low = advance(jnp.concatenate([low, past], axis=0), 1 + s, HALO)
            past = high_past[s].reshape(2, SUB, LANE)
            high = advance(jnp.concatenate([past, high], axis=0), HIGH - 1 - s, HALO)
            return low, high

        low, high = lax.fori_loop(0, STEPS, one, (low, high))
        put_rows(ua, HALO, low)
        put_rows(ua, HIGH - HALO, high)

    carry_on()
    inner()
    for pair in straight:
        wait_both_recv(pair)
    coefs(1, HALO + 1)
    coefs(HIGH, ALL - 1)
    outer(rows_of(base.at[3], 0, HALO), rows_of(base.at[3], HIGH, HALO))

    for h in range(2):
        gathered[h] = rows_of(ua, HALO + h * LEVELS, LEVELS)

    def regroup(src, dst, h, sems):
        def one(shift, carry):
            peer = lax.rem(mine + shift, LEVELS)
            pltpu.make_async_remote_copy(
                src_ref=src.at[h, peer], dst_ref=dst.at[h, mine],
                send_sem=sems.at[0, h], recv_sem=sems.at[1, h],
                device_id={"lev": which * LEVELS + peer}, device_id_type=MESH,
            ).start()
            return carry

        pltpu.make_async_copy(src.at[h, mine], dst.at[h, mine], sems.at[1, h]).start()
        lax.fori_loop(1, LEVELS, one, 0)

    def wait_half(ref, h, sem):
        pltpu.make_async_copy(ref.at[h], ref.at[h], sem).wait()

    for h in range(2):
        regroup(gathered, column, h, all_sem.at[0])
    region_copy.wait()

    wide = 2 * LANE
    column2 = column.reshape(2 * LEVELS * SUB, LANE)
    mixed2 = mixed.reshape(2 * LEVELS * SUB, LANE)

    def mix(i, carry):
        h = i // (SUB // 2)
        c = 2 * lax.rem(i, SUB // 2)
        start = h * LEVELS * SUB + c
        x = jnp.concatenate(
            [column2[pl.ds(start + q, LEVELS, stride=SUB), :] for q in range(2)], axis=1
        )
        one, two, three = thirds(x)
        stacked = jnp.concatenate([one, two, one, three, two, one], axis=0)
        every = jnp.dot(weights[...], stacked, preferred_element_type=F32)
        ids = region[h, :, pl.ds(pl.multiple_of(c * LANE, wide), wide)]
        ids = jnp.broadcast_to(ids, (LEVELS, wide))
        y = every[:LEVELS]
        for r in range(1, REGIONS):
            y = jnp.where(ids == r, every[r * LEVELS : (r + 1) * LEVELS], y)
        for q in range(2):
            mixed2[pl.ds(start + q, LEVELS, stride=SUB), :] = y[:, q * LANE : (q + 1) * LANE]
        return carry

    for h in range(2):
        wait_half(column, h, all_sem.at[0, 1, h])
        lax.fori_loop(h * SUB // 2, (h + 1) * SUB // 2, mix, 0)
        regroup(mixed, returned, h, all_sem.at[1])
    for h in range(2):
        wait_half(returned, h, all_sem.at[1, 1, h])

    for h in range(2):
        o = rows_of(base.at[2], HALO + h * LEVELS, LEVELS)
        put_rows(ua, HALO + h * LEVELS, o * returned[h])

    sent[0] = ua[SUB * HALO : 2 * SUB * HALO, :]
    sent[1] = ua[SUB * (HIGH - HALO) : SUB * HIGH, :]
    swap = tuple(
        pltpu.make_async_remote_copy(
            src_ref=sent.at[side], dst_ref=got.at[1 - side],
            send_sem=swap_send.at[side], recv_sem=swap_recv.at[side],
            device_id={"tile": tile + 2 * side - 1}, device_id_type=MESH,
        )
        for side in range(2)
    )
    start_both(swap)
    inner()
    wait_both_recv(swap)
    outer(got[0].reshape(HALO, SUB, LANE), got[1].reshape(HALO, SUB, LANE))

    def finish(block, carry):
        r = pl.multiple_of(block * SUB, SUB)
        for c in range(SUB):
            at = (pl.ds(r, SUB), slice(c * LANE, (c + 1) * LANE))
            out_ref[at] = gain[at] * ua[pl.ds((HALO + r) * SUB + c, SUB, stride=SUB), :]
        return carry

    lax.fori_loop(0, ROWS // SUB, finish, 0)

    for ref, sems in ((gathered, all_sem.at[0]), (mixed, all_sem.at[1])):
        for h in range(2):
            part = ref.at[h, pl.ds(0, LEVELS - 1)]
            pltpu.make_async_copy(part, part, sems.at[0, h]).wait()
    for pair in straight:
        wait_both_send(pair)
    wait_both_send(swap)
    for side, carrier in enumerate((down_carrier, up_carrier)):
        pl.when(carrier)(forward(side).wait_send)


def body(*args):
    raw = pltpu.VMEM((ROWS, COLS), F32)
    field = pltpu.VMEM((ALL * SUB, LANE), F32)
    slots = pltpu.VMEM((2, HALO * SUB, LANE), F32)
    cube = pltpu.VMEM((2, LEVELS, SUB, LANE), F32)
    out = pl.pallas_call(
        kernel,
        out_shape=jax.ShapeDtypeStruct((ROWS, COLS), F32),
        in_specs=[pl.BlockSpec(memory_space=pltpu.HBM)] * 7,
        out_specs=pl.BlockSpec(memory_space=pltpu.VMEM),
        scratch_shapes=[
            raw, raw, raw, raw,
            pltpu.VMEM((ROWS, COLS), jnp.int32),
            pltpu.VMEM((2, 1, COLS), jnp.int32),
            pltpu.VMEM((REGIONS, LEVELS, LEVELS), F32),
            pltpu.VMEM((4, ALL * SUB, LANE), F32),
            field, field, field, field, field, field, field,
            pltpu.VMEM((HALO, 2 * SUB, LANE), F32),
            pltpu.VMEM((HALO, 2 * SUB, LANE), F32),
            slots, slots, slots,
            cube, cube, cube, cube,
            pltpu.VMEM((REGIONS * LEVELS, LEVELS), F32),
            pltpu.VMEM((REGIONS * LEVELS, 6 * LEVELS), BF16),
            pltpu.SemaphoreType.DMA((7,)),
            pltpu.SemaphoreType.DMA((2, 4)),
            pltpu.SemaphoreType.DMA((2, 4)),
            pltpu.SemaphoreType.DMA((2,)),
            pltpu.SemaphoreType.DMA((2,)),
            pltpu.SemaphoreType.DMA((2,)),
            pltpu.SemaphoreType.DMA((2,)),
            pltpu.SemaphoreType.DMA((2,)),
            pltpu.SemaphoreType.DMA((2, 2, 2)),
        ],
        compiler_params=pltpu.CompilerParams(
            collective_id=0, has_side_effects=True, vmem_limit_bytes=32 * 1024 * 1024
        ),
        name="covariance",
    )(*[pltpu.with_memory_space_constraint(x, pltpu.HBM) for x in args])
    return out[None]


def solution(mesh):
    return jax.shard_map(
        body,
        mesh=mesh,
        in_specs=(
            P("lev", "tile", None),
            P("lev", "tile", None),
            P("lev", "tile", None),
            P("lev", "tile", None),
            P("lev", "tile", None),
            P(("tile", "lev"), None),
            P(),
        ),
        out_specs=P("lev", "tile", None),
        check_vma=False,
    )
```

```python
import functools

import jax
import jax.numpy as jnp
from jax import lax
from jax.experimental import pallas as pl
from jax.experimental.pallas import tpu as pltpu
from jax.sharding import PartitionSpec as P

FIELDS = 2
LEVELS = 32
STEPS = 10
REGIONS = 16
ROWS = 64
COLS = 1024
SUB = 8
LANE = 128
EDGE = 16
HALO = 10
HIGH = HALO + ROWS
ALL = HALO + ROWS + HALO
WIDE = 4
BLOCK = 14
MESH = pl.DeviceIdType.MESH
F32 = jnp.float32
BF16 = jnp.bfloat16


def rows_of(ref, start, count):
    return ref[pl.ds(SUB * start, SUB * count), :].reshape(count, SUB, LANE)


def put_rows(ref, start, value):
    count = value.shape[0]
    ref[pl.ds(SUB * start, SUB * count), :] = value.reshape(count * SUB, LANE)


def east_of(x, lane):
    near = pltpu.roll(x, LANE - 1, 2)
    return jnp.where(lane == LANE - 1, pltpu.roll(near, SUB - 1, 1), near)


def west_of(x, lane):
    near = pltpu.roll(x, 1, 2)
    return jnp.where(lane == 0, pltpu.roll(near, 1, 1), near)


def kernel(
    control_hbm, gain_hbm, north_hbm, east_hbm, land_hbm, region_hbm, tiles_hbm,
    out_ref,
    control, gain, north, east, land, own_region, region, tiles,
    base, ua, ub, ca, cn, cs, ce, cw,
    low_past, high_past, carried, sent, got, gathered, column, mixed, returned,
    product, weights,
    in_sem, halo_send, halo_recv, carry_recv, carry_send, swap_send, swap_recv, region_sem, all_sem,
):
    tile = lax.axis_index("tile")
    lev = lax.axis_index("lev")
    tile_count = lax.axis_size("tile")
    which = lev // LEVELS
    mine = lax.rem(lev, LEVELS)
    last = tile_count - 1
    place = lax.rem(tile, WIDE)
    band = tile // WIDE
    bands = tile_count // WIDE
    upper_end = jnp.logical_and(place == WIDE - 1, band < bands - 1)
    lower_end = jnp.logical_and(place == 0, band > 0)
    down_carrier = jnp.logical_and(place > 0, band > 0)
    up_carrier = jnp.logical_and(place < WIDE - 1, band < bands - 1)

    loads = [
        pltpu.make_async_copy(land_hbm.at[0], land, in_sem.at[0]),
        pltpu.make_async_copy(north_hbm.at[0], north, in_sem.at[1]),
        pltpu.make_async_copy(east_hbm.at[0], east, in_sem.at[2]),
        pltpu.make_async_copy(gain_hbm.at[0], gain, in_sem.at[3]),
        pltpu.make_async_copy(control_hbm.at[0], control, in_sem.at[4]),
        pltpu.make_async_copy(region_hbm, own_region, in_sem.at[5]),
        pltpu.make_async_copy(tiles_hbm.at[:, which], tiles, in_sem.at[6]),
    ]
    for load in loads:
        load.start()

    barrier = pltpu.get_barrier_semaphore()

    def group_peer(shift):
        return which * LEVELS + lax.rem(mine + shift, LEVELS)

    @pl.when(tile > 0)
    def _():
        pl.semaphore_signal(barrier, inc=1, device_id={"tile": tile - 1}, device_id_type=MESH)

    @pl.when(tile < last)
    def _():
        pl.semaphore_signal(barrier, inc=1, device_id={"tile": tile + 1}, device_id_type=MESH)

    for far in range(1, WIDE):
        for end, offset in ((upper_end, far + 1), (lower_end, far), (lower_end, -far - 1), (upper_end, -far)):
            @pl.when(end)
            def _(offset=offset):
                pl.semaphore_signal(barrier, inc=1, device_id={"tile": tile + offset}, device_id_type=MESH)

    for carrier, offset in (
        (down_carrier, -place - 1), (down_carrier, -place),
        (up_carrier, WIDE - place), (up_carrier, WIDE - 1 - place),
    ):
        @pl.when(carrier)
        def _(offset=offset):
            pl.semaphore_signal(barrier, inc=1, device_id={"tile": tile + offset}, device_id_type=MESH)

    partner = lax.rem(lev + LEVELS, FIELDS * LEVELS)
    pl.semaphore_signal(barrier, inc=1, device_id={"lev": partner}, device_id_type=MESH)
    middle = jnp.logical_and(lev >= EDGE, lev < ROWS - EDGE)

    @pl.when(middle)
    def _():
        other = lev + EDGE - 2 * EDGE * which
        pl.semaphore_signal(barrier, inc=1, device_id={"lev": other}, device_id_type=MESH)


    def greet(shift, carry):
        pl.semaphore_signal(barrier, inc=1, device_id={"lev": group_peer(shift)}, device_id_type=MESH)
        return carry

    lax.fori_loop(1, LEVELS, greet, 0)

    for load in loads[:5]:
        load.wait()

    def relayout(block, carry):
        r = pl.multiple_of(block * SUB, SUB)
        for c in range(SUB):
            at = (pl.ds(r, SUB), slice(c * LANE, (c + 1) * LANE))
            to = pl.ds((HALO + r) * SUB + c, SUB, stride=SUB)
            ocean = land[at].astype(F32)
            base[0, to, :] = north[at]
            base[1, to, :] = east[at]
            base[2, to, :] = ocean
            start = ocean * gain[at] * control[at]
            base[3, to, :] = start
            ua[to, :] = start
        return carry

    lax.fori_loop(0, ROWS // SUB, relayout, 0)
    loads[5].wait()

    def as_count(flag):
        return flag.astype(jnp.int32)

    greeted = LEVELS + as_count(middle) + as_count(tile > 0) + as_count(tile < last)
    greeted = greeted + 2 * (WIDE - 1) * (as_count(upper_end) + as_count(lower_end))
    greeted = greeted + 2 * (as_count(up_carrier) + as_count(down_carrier))
    pl.semaphore_wait(barrier, greeted)

    def rim(a, start):
        return base.at[a, pl.ds(SUB * start, SUB * HALO), :]

    def send_rim(a, side, offset, to=None):
        start, land_at = ((HALO, HIGH), (HIGH - HALO, 0))[side]
        return pltpu.make_async_remote_copy(
            src_ref=rim(a, start), dst_ref=rim(a, land_at) if to is None else to,
            send_sem=halo_send.at[side, a],
            recv_sem=halo_recv.at[side, a] if to is None else carry_recv.at[side],
            device_id={"tile": tile + offset}, device_id_type=MESH,
        )

    def forward(side):
        a = (place - 1, WIDE - 2 - place)[side]
        return pltpu.make_async_remote_copy(
            src_ref=carried.at[side], dst_ref=rim(a, (HIGH, 0)[side]),
            send_sem=carry_send.at[side], recv_sem=halo_recv.at[side, a],
            device_id={"tile": tile + (-place - 1, WIDE - place)[side]}, device_id_type=MESH,
        )

    has_lower, has_upper = tile > 0, tile < last

    def start_both(pair):
        pl.when(has_lower)(pair[0].start)
        pl.when(has_upper)(pair[1].start)

    def wait_both_recv(pair):
        pl.when(has_upper)(pair[0].wait_recv)
        pl.when(has_lower)(pair[1].wait_recv)

    def wait_both_send(pair):
        pl.when(has_lower)(pair[0].wait_send)
        pl.when(has_upper)(pair[1].wait_send)

    straight = [(send_rim(a, 0, -1), send_rim(a, 1, 1)) for a in range(4)]
    for a in range(WIDE - 1):
        pl.when(lower_end)(send_rim(a, 0, 1 + a, carried.at[0]).start)
        pl.when(upper_end)(send_rim(a, 1, -1 - a, carried.at[1]).start)
    start_both(straight[3])
    for a in range(WIDE - 1):
        pl.when(jnp.logical_and(has_lower, jnp.logical_not(lower_end)))(straight[a][0].start)
        pl.when(jnp.logical_and(has_upper, jnp.logical_not(upper_end)))(straight[a][1].start)

    def carry_on():
        for side, carrier in enumerate((down_carrier, up_carrier)):
            @pl.when(carrier)
            def _(side=side):
                copy = forward(side)
                pltpu.make_async_copy(carried.at[side], carried.at[side], carry_recv.at[side]).wait()
                copy.start()

    def send_region(slot, to, send):
        return pltpu.make_async_remote_copy(
            src_ref=own_region, dst_ref=region.at[slot],
            send_sem=region_sem.at[send], recv_sem=region_sem.at[2 + slot],
            device_id={"lev": to}, device_id_type=MESH,
        )

    outer_region = send_region(0, partner, 0)
    inner_regions = send_region(1, lev - EDGE, 0), send_region(1, lev + EDGE, 1)

    @pl.when(middle)
    def _():
        for copy in inner_regions:
            copy.start()

    @pl.when(jnp.logical_not(middle))
    def _():
        outer_region.start()
        region[0] = own_region[...]

    @pl.when(tile == 0)
    def _():
        for a in range(4):
            base[a, : SUB * HALO, :] = jnp.zeros((SUB * HALO, LANE), F32)
        got[0] = jnp.zeros(got.shape[1:], F32)

    @pl.when(tile == last)
    def _():
        for a in range(4):
            base[a, SUB * HIGH :, :] = jnp.zeros((SUB * HALO, LANE), F32)
        got[1] = jnp.zeros(got.shape[1:], F32)

    first_lane = (1, SUB, LANE)
    lane1 = lax.broadcasted_iota(jnp.int32, first_lane, 2)
    sub1 = lax.broadcasted_iota(jnp.int32, first_lane, 1)
    west_edge = jnp.logical_and(lane1 == 0, sub1 == 0)
    east_edge = jnp.logical_and(lane1 == LANE - 1, sub1 == SUB - 1)

    def make_coef(start, count):
        shape = (count, SUB, LANE)
        lane = jnp.broadcast_to(lane1, shape)
        n = rows_of(base.at[0], start, count)
        s = rows_of(base.at[0], start - 1, count)
        e = rows_of(base.at[1], start, count)
        o = rows_of(base.at[2], start, count)
        w = jnp.where(west_edge, 0.0, west_of(e, lane))
        put_rows(ca, start, o * (1.0 - n - s - e - w))
        put_rows(cn, start, o * n)
        put_rows(cs, start, o * s)
        put_rows(ce, start, o * jnp.where(east_edge, 0.0, e))
        put_rows(cw, start, o * w)

    def coefs(start, end):
        for at in range(start, end, BLOCK):
            make_coef(at, min(BLOCK, end - at))

    def coef_block(b, carry):
        make_coef(HALO + 1 + b * 9, 9)
        return carry

    lax.fori_loop(0, (ROWS - 1) // 9, coef_block, 0)

    def advance(wide, start, count):
        lane = jnp.broadcast_to(lane1, (count, SUB, LANE))
        u = wide[1:-1]
        v = rows_of(ca, start, count) * u
        v = v + rows_of(cn, start, count) * wide[2:]
        v = v + rows_of(cs, start, count) * wide[:-2]
        v = v + rows_of(ce, start, count) * east_of(u, lane)
        return v + rows_of(cw, start, count) * west_of(u, lane)

    def inner_step(src, dst, s):
        low_past[s] = src[pl.ds(SUB * (HALO + s), 2 * SUB), :]
        high_past[s] = src[pl.ds(SUB * (HIGH - 2 - s), 2 * SUB), :]
        at, end = HALO + 1, HIGH - 1
        while at < end:
            count = min(BLOCK, end - at)
            put_rows(dst, at, advance(rows_of(src, at - 1, count + 2), at, count))
            at += count

    def inner():
        def pair(i, carry):
            inner_step(ua, ub, 2 * i)
            inner_step(ub, ua, 2 * i + 1)
            return carry

        lax.fori_loop(0, STEPS // 2, pair, 0)

    def outer(low, high):
        def one(s, carry):
            low, high = carry
            past = low_past[s].reshape(2, SUB, LANE)
            low = advance(jnp.concatenate([low, past], axis=0), 1 + s, HALO)
            past = high_past[s].reshape(2, SUB, LANE)
            high = advance(jnp.concatenate([past, high], axis=0), HIGH - 1 - s, HALO)
            return low, high

        low, high = lax.fori_loop(0, STEPS, one, (low, high))
        put_rows(ua, HALO, low)
        put_rows(ua, HIGH - HALO, high)

    def regroup(src, dst, h, sems):
        def one(shift, carry):
            peer = lax.rem(mine + shift, LEVELS)
            pltpu.make_async_remote_copy(
                src_ref=src.at[h, peer], dst_ref=dst.at[h, mine],
                send_sem=sems.at[0, h], recv_sem=sems.at[1, h],
                device_id={"lev": which * LEVELS + peer}, device_id_type=MESH,
            ).start()
            return carry

        pltpu.make_async_copy(src.at[h, mine], dst.at[h, mine], sems.at[1, h]).start()
        lax.fori_loop(1, LEVELS, one, 0)

    def wait_half(ref, h, sem):
        pltpu.make_async_copy(ref.at[h], ref.at[h], sem).wait()

    wide = 2 * LANE
    column2 = column.reshape(2 * LEVELS * SUB, LANE)
    mixed2 = mixed.reshape(2 * LEVELS * SUB, LANE)

    def mix(i, carry):
        h = i // (SUB // 2)
        c = 2 * lax.rem(i, SUB // 2)
        start = h * LEVELS * SUB + c
        x = jnp.concatenate(
            [column2[pl.ds(start + q, LEVELS, stride=SUB), :] for q in range(2)], axis=1
        )
        one, two, three = thirds(x)
        stacked = jnp.concatenate([one, two, one, three, two, one], axis=0)
        every = jnp.dot(weights[...], stacked, preferred_element_type=F32)
        ids = region[h, :, pl.ds(pl.multiple_of(c * LANE, wide), wide)]
        ids = jnp.broadcast_to(ids, (LEVELS, wide))
        y = every[:LEVELS]
        for r in range(1, REGIONS):
            y = jnp.where(ids == r, every[r * LEVELS : (r + 1) * LEVELS], y)
        for q in range(2):
            mixed2[pl.ds(start + q, LEVELS, stride=SUB), :] = y[:, q * LANE : (q + 1) * LANE]
        return carry

    def blend(h):
        wait_half(column, h, all_sem.at[0, 1, h])
        lax.fori_loop(h * SUB // 2, (h + 1) * SUB // 2, mix, 0)

    carry_on()
    inner()
    gathered[1] = rows_of(ua, HALO + EDGE, LEVELS)
    regroup(gathered, column, 1, all_sem.at[0])

    loads[6].wait()

    def square(r, carry):
        t = tiles[r]
        m = lax.dot_general(
            t, t, (((0,), (0,)), ((), ())), precision=lax.Precision.HIGHEST, preferred_element_type=F32
        )
        product[pl.ds(pl.multiple_of(r * LEVELS, LEVELS), LEVELS), :] = m
        return carry

    lax.fori_loop(0, REGIONS, square, 0, unroll=True)

    def thirds(x):
        one = x.astype(BF16)
        rest = x - one.astype(F32)
        two = rest.astype(BF16)
        three = (rest - two.astype(F32)).astype(BF16)
        return one, two, three

    k_of = lax.broadcasted_iota(jnp.int32, (LEVELS, 6 * LEVELS), 0)
    j_of = lax.broadcasted_iota(jnp.int32, (LEVELS, 6 * LEVELS), 1)
    total = None
    for part, groups in zip(thirds(product[...]), ((0, 1, 3), (2, 4), (5,))):
        pick = jnp.zeros((LEVELS, 6 * LEVELS), F32)
        for g in groups:
            pick = pick + jnp.where(j_of == k_of + g * LEVELS, 1.0, 0.0)
        spread = jnp.dot(part, pick.astype(BF16), preferred_element_type=F32)
        total = spread if total is None else total + spread
    weights[...] = total.astype(BF16)
    for pair in straight:
        wait_both_recv(pair)
    coefs(1, HALO + 1)
    coefs(HIGH, ALL - 1)
    outer(rows_of(base.at[3], 0, HALO), rows_of(base.at[3], HIGH, HALO))
    gathered[0, :EDGE] = rows_of(ua, HALO, EDGE)
    gathered[0, EDGE:] = rows_of(ua, HIGH - EDGE, EDGE)
    regroup(gathered, column, 0, all_sem.at[0])
    inner_regions[0].wait_recv()
    blend(1)
    pl.when(middle)(outer_region.wait_recv)
    blend(0)
    regroup(mixed, returned, 0, all_sem.at[1])
    regroup(mixed, returned, 1, all_sem.at[1])

    def take(h, first, start, count):
        o = rows_of(base.at[2], HALO + start, count)
        put_rows(ua, HALO + start, o * returned[h, first : first + count])

    wait_half(returned, 0, all_sem.at[1, 1, 0])
    take(0, 0, 0, EDGE)
    take(0, EDGE, ROWS - EDGE, EDGE)
    sent[0] = ua[SUB * HALO : 2 * SUB * HALO, :]
    sent[1] = ua[SUB * (HIGH - HALO) : SUB * HIGH, :]
    swap = tuple(
        pltpu.make_async_remote_copy(
            src_ref=sent.at[side], dst_ref=got.at[1 - side],
            send_sem=swap_send.at[side], recv_sem=swap_recv.at[side],
            device_id={"tile": tile + 2 * side - 1}, device_id_type=MESH,
        )
        for side in range(2)
    )
    start_both(swap)
    wait_half(returned, 1, all_sem.at[1, 1, 1])
    take(1, 0, EDGE, LEVELS)
    inner()
    wait_both_recv(swap)
    outer(got[0].reshape(HALO, SUB, LANE), got[1].reshape(HALO, SUB, LANE))

    def finish(block, carry):
        r = pl.multiple_of(block * SUB, SUB)
        for c in range(SUB):
            at = (pl.ds(r, SUB), slice(c * LANE, (c + 1) * LANE))
            out_ref[at] = gain[at] * ua[pl.ds((HALO + r) * SUB + c, SUB, stride=SUB), :]
        return carry

    lax.fori_loop(0, ROWS // SUB, finish, 0)

    for ref, sems in ((gathered, all_sem.at[0]), (mixed, all_sem.at[1])):
        for h in range(2):
            part = ref.at[h, pl.ds(0, LEVELS - 1)]
            pltpu.make_async_copy(part, part, sems.at[0, h]).wait()
    for pair in straight:
        wait_both_send(pair)
    wait_both_send(swap)
    inner_regions[0].wait_send()
    pl.when(middle)(inner_regions[1].wait_send)
    for side, carrier in enumerate((down_carrier, up_carrier)):
        pl.when(carrier)(forward(side).wait_send)


def body(*args):
    raw = pltpu.VMEM((ROWS, COLS), F32)
    field = pltpu.VMEM((ALL * SUB, LANE), F32)
    slots = pltpu.VMEM((2, HALO * SUB, LANE), F32)
    cube = pltpu.VMEM((2, LEVELS, SUB, LANE), F32)
    out = pl.pallas_call(
        kernel,
        out_shape=jax.ShapeDtypeStruct((ROWS, COLS), F32),
        in_specs=[pl.BlockSpec(memory_space=pltpu.HBM)] * 7,
        out_specs=pl.BlockSpec(memory_space=pltpu.VMEM),
        scratch_shapes=[
            raw, raw, raw, raw,
            pltpu.VMEM((ROWS, COLS), jnp.int32),
            pltpu.VMEM((1, COLS), jnp.int32),
            pltpu.VMEM((2, 1, COLS), jnp.int32),
            pltpu.VMEM((REGIONS, LEVELS, LEVELS), F32),
            pltpu.VMEM((4, ALL * SUB, LANE), F32),
            field, field, field, field, field, field, field,
            pltpu.VMEM((HALO, 2 * SUB, LANE), F32),
            pltpu.VMEM((HALO, 2 * SUB, LANE), F32),
            slots, slots, slots,
            cube, cube, cube, cube,
            pltpu.VMEM((REGIONS * LEVELS, LEVELS), F32),
            pltpu.VMEM((REGIONS * LEVELS, 6 * LEVELS), BF16),
            pltpu.SemaphoreType.DMA((7,)),
            pltpu.SemaphoreType.DMA((2, 4)),
            pltpu.SemaphoreType.DMA((2, 4)),
            pltpu.SemaphoreType.DMA((2,)),
            pltpu.SemaphoreType.DMA((2,)),
            pltpu.SemaphoreType.DMA((2,)),
            pltpu.SemaphoreType.DMA((2,)),
            pltpu.SemaphoreType.DMA((4,)),
            pltpu.SemaphoreType.DMA((2, 2, 2)),
        ],
        compiler_params=pltpu.CompilerParams(
            collective_id=0, has_side_effects=True, vmem_limit_bytes=32 * 1024 * 1024
        ),
        name="covariance",
    )(*[pltpu.with_memory_space_constraint(x, pltpu.HBM) for x in args])
    return out[None]


def solution(mesh):
    return jax.shard_map(
        body,
        mesh=mesh,
        in_specs=(
            P("lev", "tile", None),
            P("lev", "tile", None),
            P("lev", "tile", None),
            P("lev", "tile", None),
            P("lev", "tile", None),
            P(("tile", "lev"), None),
            P(),
        ),
        out_specs=P("lev", "tile", None),
        check_vma=False,
    )
```

```python
import functools

import jax
import jax.numpy as jnp
from jax import lax
from jax.experimental import pallas as pl
from jax.experimental.pallas import tpu as pltpu
from jax.sharding import PartitionSpec as P

FIELDS = 2
LEVELS = 32
STEPS = 10
REGIONS = 16
ROWS = 64
COLS = 1024
SUB = 8
LANE = 128
EDGE = 16
HALO = 10
HIGH = HALO + ROWS
ALL = HALO + ROWS + HALO
WIDE = 4
BLOCK = 14
MESH = pl.DeviceIdType.MESH
F32 = jnp.float32
BF16 = jnp.bfloat16


def rows_of(ref, start, count):
    return ref[pl.ds(SUB * start, SUB * count), :].reshape(count, SUB, LANE)


def put_rows(ref, start, value):
    count = value.shape[0]
    ref[pl.ds(SUB * start, SUB * count), :] = value.reshape(count * SUB, LANE)


def east_of(x, lane):
    near = pltpu.roll(x, LANE - 1, 2)
    return jnp.where(lane == LANE - 1, pltpu.roll(near, SUB - 1, 1), near)


def west_of(x, lane):
    near = pltpu.roll(x, 1, 2)
    return jnp.where(lane == 0, pltpu.roll(near, 1, 1), near)


def kernel(
    control_hbm, gain_hbm, north_hbm, east_hbm, land_hbm, region_hbm, tiles_hbm,
    out_ref,
    control, gain, north, east, land, own_region, region, tiles,
    base, ua, ub, ca, cn, cs, ce, cw,
    low_past, high_past, carried, sent, got, gathered, column, mixed, returned,
    product, weights,
    in_sem, halo_send, halo_recv, carry_recv, carry_send, swap_send, swap_recv, region_sem, all_sem,
):
    tile = lax.axis_index("tile")
    lev = lax.axis_index("lev")
    tile_count = lax.axis_size("tile")
    which = lev // LEVELS
    mine = lax.rem(lev, LEVELS)
    last = tile_count - 1
    place = lax.rem(tile, WIDE)
    band = tile // WIDE
    bands = tile_count // WIDE
    upper_end = jnp.logical_and(place == WIDE - 1, band < bands - 1)
    lower_end = jnp.logical_and(place == 0, band > 0)
    down_carrier = jnp.logical_and(place > 0, band > 0)
    up_carrier = jnp.logical_and(place < WIDE - 1, band < bands - 1)

    loads = [
        pltpu.make_async_copy(land_hbm.at[0], land, in_sem.at[0]),
        pltpu.make_async_copy(north_hbm.at[0], north, in_sem.at[1]),
        pltpu.make_async_copy(east_hbm.at[0], east, in_sem.at[2]),
        pltpu.make_async_copy(gain_hbm.at[0], gain, in_sem.at[3]),
        pltpu.make_async_copy(control_hbm.at[0], control, in_sem.at[4]),
        pltpu.make_async_copy(region_hbm, own_region, in_sem.at[5]),
        pltpu.make_async_copy(tiles_hbm.at[:, which], tiles, in_sem.at[6]),
    ]
    for load in loads:
        load.start()

    barrier = pltpu.get_barrier_semaphore()

    def group_peer(shift):
        return which * LEVELS + lax.rem(mine + shift, LEVELS)

    @pl.when(tile > 0)
    def _():
        pl.semaphore_signal(barrier, inc=1, device_id={"tile": tile - 1}, device_id_type=MESH)

    @pl.when(tile < last)
    def _():
        pl.semaphore_signal(barrier, inc=1, device_id={"tile": tile + 1}, device_id_type=MESH)

    for far in range(1, WIDE):
        for end, offset in ((upper_end, far + 1), (lower_end, far), (lower_end, -far - 1), (upper_end, -far)):
            @pl.when(end)
            def _(offset=offset):
                pl.semaphore_signal(barrier, inc=1, device_id={"tile": tile + offset}, device_id_type=MESH)

    for carrier, offset in (
        (down_carrier, -place - 1), (down_carrier, -place),
        (up_carrier, WIDE - place), (up_carrier, WIDE - 1 - place),
    ):
        @pl.when(carrier)
        def _(offset=offset):
            pl.semaphore_signal(barrier, inc=1, device_id={"tile": tile + offset}, device_id_type=MESH)

    partner = lax.rem(lev + LEVELS, FIELDS * LEVELS)
    pl.semaphore_signal(barrier, inc=1, device_id={"lev": partner}, device_id_type=MESH)
    middle = jnp.logical_and(lev >= EDGE, lev < ROWS - EDGE)

    @pl.when(middle)
    def _():
        other = lev + EDGE - 2 * EDGE * which
        pl.semaphore_signal(barrier, inc=1, device_id={"lev": other}, device_id_type=MESH)


    def greet(shift, carry):
        pl.semaphore_signal(barrier, inc=1, device_id={"lev": group_peer(shift)}, device_id_type=MESH)
        return carry

    lax.fori_loop(1, LEVELS, greet, 0)

    for load in loads[:5]:
        load.wait()

    def relayout(block, carry):
        r = pl.multiple_of(block * SUB, SUB)
        for c in range(SUB):
            at = (pl.ds(r, SUB), slice(c * LANE, (c + 1) * LANE))
            to = pl.ds((HALO + r) * SUB + c, SUB, stride=SUB)
            ocean = land[at].astype(F32)
            base[0, to, :] = north[at]
            base[1, to, :] = east[at]
            base[2, to, :] = ocean
            start = ocean * gain[at] * control[at]
            base[3, to, :] = start
            ua[to, :] = start
        return carry

    lax.fori_loop(0, ROWS // SUB, relayout, 0, unroll=True)
    loads[5].wait()

    def as_count(flag):
        return flag.astype(jnp.int32)

    greeted = LEVELS + as_count(middle) + as_count(tile > 0) + as_count(tile < last)
    greeted = greeted + 2 * (WIDE - 1) * (as_count(upper_end) + as_count(lower_end))
    greeted = greeted + 2 * (as_count(up_carrier) + as_count(down_carrier))
    pl.semaphore_wait(barrier, greeted)

    def rim(a, start):
        return base.at[a, pl.ds(SUB * start, SUB * HALO), :]

    def send_rim(a, side, offset, to=None):
        start, land_at = ((HALO, HIGH), (HIGH - HALO, 0))[side]
        return pltpu.make_async_remote_copy(
            src_ref=rim(a, start), dst_ref=rim(a, land_at) if to is None else to,
            send_sem=halo_send.at[side, a],
            recv_sem=halo_recv.at[side, a] if to is None else carry_recv.at[side],
            device_id={"tile": tile + offset}, device_id_type=MESH,
        )

    def forward(side):
        a = (place - 1, WIDE - 2 - place)[side]
        return pltpu.make_async_remote_copy(
            src_ref=carried.at[side], dst_ref=rim(a, (HIGH, 0)[side]),
            send_sem=carry_send.at[side], recv_sem=halo_recv.at[side, a],
            device_id={"tile": tile + (-place - 1, WIDE - place)[side]}, device_id_type=MESH,
        )

    has_lower, has_upper = tile > 0, tile < last

    def start_both(pair):
        pl.when(has_lower)(pair[0].start)
        pl.when(has_upper)(pair[1].start)

    def wait_both_recv(pair):
        pl.when(has_upper)(pair[0].wait_recv)
        pl.when(has_lower)(pair[1].wait_recv)

    def wait_both_send(pair):
        pl.when(has_lower)(pair[0].wait_send)
        pl.when(has_upper)(pair[1].wait_send)

    straight = [(send_rim(a, 0, -1), send_rim(a, 1, 1)) for a in range(4)]
    for a in range(WIDE - 1):
        pl.when(lower_end)(send_rim(a, 0, 1 + a, carried.at[0]).start)
        pl.when(upper_end)(send_rim(a, 1, -1 - a, carried.at[1]).start)
    start_both(straight[3])
    for a in range(WIDE - 1):
        pl.when(jnp.logical_and(has_lower, jnp.logical_not(lower_end)))(straight[a][0].start)
        pl.when(jnp.logical_and(has_upper, jnp.logical_not(upper_end)))(straight[a][1].start)

    def carry_on():
        for side, carrier in enumerate((down_carrier, up_carrier)):
            @pl.when(carrier)
            def _(side=side):
                copy = forward(side)
                pltpu.make_async_copy(carried.at[side], carried.at[side], carry_recv.at[side]).wait()
                copy.start()

    def send_region(slot, to, send):
        return pltpu.make_async_remote_copy(
            src_ref=own_region, dst_ref=region.at[slot],
            send_sem=region_sem.at[send], recv_sem=region_sem.at[2 + slot],
            device_id={"lev": to}, device_id_type=MESH,
        )

    outer_region = send_region(0, partner, 0)
    inner_regions = send_region(1, lev - EDGE, 0), send_region(1, lev + EDGE, 1)

    @pl.when(middle)
    def _():
        for copy in inner_regions:
            copy.start()

    @pl.when(jnp.logical_not(middle))
    def _():
        outer_region.start()
        region[0] = own_region[...]

    @pl.when(tile == 0)
    def _():
        for a in range(4):
            base[a, : SUB * HALO, :] = jnp.zeros((SUB * HALO, LANE), F32)
        got[0] = jnp.zeros(got.shape[1:], F32)

    @pl.when(tile == last)
    def _():
        for a in range(4):
            base[a, SUB * HIGH :, :] = jnp.zeros((SUB * HALO, LANE), F32)
        got[1] = jnp.zeros(got.shape[1:], F32)

    first_lane = (1, SUB, LANE)
    lane1 = lax.broadcasted_iota(jnp.int32, first_lane, 2)
    sub1 = lax.broadcasted_iota(jnp.int32, first_lane, 1)
    west_edge = jnp.logical_and(lane1 == 0, sub1 == 0)
    east_edge = jnp.logical_and(lane1 == LANE - 1, sub1 == SUB - 1)

    def make_coef(start, count):
        shape = (count, SUB, LANE)
        lane = jnp.broadcast_to(lane1, shape)
        n = rows_of(base.at[0], start, count)
        s = rows_of(base.at[0], start - 1, count)
        e = rows_of(base.at[1], start, count)
        o = rows_of(base.at[2], start, count)
        w = jnp.where(west_edge, 0.0, west_of(e, lane))
        put_rows(ca, start, o * (1.0 - n - s - e - w))
        put_rows(cn, start, o * n)
        put_rows(cs, start, o * s)
        put_rows(ce, start, o * jnp.where(east_edge, 0.0, e))
        put_rows(cw, start, o * w)

    def coefs(start, end):
        for at in range(start, end, BLOCK):
            make_coef(at, min(BLOCK, end - at))

    def coef_block(b, carry):
        make_coef(HALO + 1 + b * 9, 9)
        return carry

    lax.fori_loop(0, (ROWS - 1) // 9, coef_block, 0)

    def advance(wide, start, count):
        lane = jnp.broadcast_to(lane1, (count, SUB, LANE))
        u = wide[1:-1]
        v = rows_of(ca, start, count) * u
        v = v + rows_of(cn, start, count) * wide[2:]
        v = v + rows_of(cs, start, count) * wide[:-2]
        v = v + rows_of(ce, start, count) * east_of(u, lane)
        return v + rows_of(cw, start, count) * west_of(u, lane)

    def inner_step(src, dst, s):
        low_past[s] = src[pl.ds(SUB * (HALO + s), 2 * SUB), :]
        high_past[s] = src[pl.ds(SUB * (HIGH - 2 - s), 2 * SUB), :]
        at, end = HALO + 1, HIGH - 1
        while at < end:
            count = min(BLOCK, end - at)
            put_rows(dst, at, advance(rows_of(src, at - 1, count + 2), at, count))
            at += count

    def inner():
        def pair(i, carry):
            inner_step(ua, ub, 2 * i)
            inner_step(ub, ua, 2 * i + 1)
            return carry

        lax.fori_loop(0, STEPS // 2, pair, 0)

    def outer(low, high):
        def one(s, carry):
            low, high = carry
            past = low_past[s].reshape(2, SUB, LANE)
            low = advance(jnp.concatenate([low, past], axis=0), 1 + s, HALO)
            past = high_past[s].reshape(2, SUB, LANE)
            high = advance(jnp.concatenate([past, high], axis=0), HIGH - 1 - s, HALO)
            return low, high

        low, high = lax.fori_loop(0, STEPS, one, (low, high))
        put_rows(ua, HALO, low)
        put_rows(ua, HIGH - HALO, high)

    def regroup(src, dst, h, sems):
        def one(shift, carry):
            peer = lax.rem(mine + shift, LEVELS)
            pltpu.make_async_remote_copy(
                src_ref=src.at[h, peer], dst_ref=dst.at[h, mine],
                send_sem=sems.at[0, h], recv_sem=sems.at[1, h],
                device_id={"lev": which * LEVELS + peer}, device_id_type=MESH,
            ).start()
            return carry

        pltpu.make_async_copy(src.at[h, mine], dst.at[h, mine], sems.at[1, h]).start()
        lax.fori_loop(1, LEVELS, one, 0)

    def wait_half(ref, h, sem):
        pltpu.make_async_copy(ref.at[h], ref.at[h], sem).wait()

    wide = 2 * LANE
    column2 = column.reshape(2 * LEVELS * SUB, LANE)
    mixed2 = mixed.reshape(2 * LEVELS * SUB, LANE)

    def mix(i, carry):
        h = i // (SUB // 2)
        c = 2 * lax.rem(i, SUB // 2)
        start = h * LEVELS * SUB + c
        x = jnp.concatenate(
            [column2[pl.ds(start + q, LEVELS, stride=SUB), :] for q in range(2)], axis=1
        )
        one, two, three = thirds(x)
        stacked = jnp.concatenate([one, two, one, three, two, one], axis=0)
        every = jnp.dot(weights[...], stacked, preferred_element_type=F32)
        ids = region[h, :, pl.ds(pl.multiple_of(c * LANE, wide), wide)]
        ids = jnp.broadcast_to(ids, (LEVELS, wide))
        y = every[:LEVELS]
        for r in range(1, REGIONS):
            y = jnp.where(ids == r, every[r * LEVELS : (r + 1) * LEVELS], y)
        for q in range(2):
            mixed2[pl.ds(start + q, LEVELS, stride=SUB), :] = y[:, q * LANE : (q + 1) * LANE]
        return carry

    def blend(h):
        wait_half(column, h, all_sem.at[0, 1, h])
        lax.fori_loop(h * SUB // 2, (h + 1) * SUB // 2, mix, 0, unroll=True)

    carry_on()
    inner()
    gathered[1] = rows_of(ua, HALO + EDGE, LEVELS)
    regroup(gathered, column, 1, all_sem.at[0])

    loads[6].wait()

    def square(r, carry):
        t = tiles[r]
        m = lax.dot_general(
            t, t, (((0,), (0,)), ((), ())), precision=lax.Precision.HIGHEST, preferred_element_type=F32
        )
        product[pl.ds(pl.multiple_of(r * LEVELS, LEVELS), LEVELS), :] = m
        return carry

    lax.fori_loop(0, REGIONS, square, 0, unroll=True)

    def thirds(x):
        one = x.astype(BF16)
        rest = x - one.astype(F32)
        two = rest.astype(BF16)
        three = (rest - two.astype(F32)).astype(BF16)
        return one, two, three

    k_of = lax.broadcasted_iota(jnp.int32, (LEVELS, 6 * LEVELS), 0)
    j_of = lax.broadcasted_iota(jnp.int32, (LEVELS, 6 * LEVELS), 1)
    total = None
    for part, groups in zip(thirds(product[...]), ((0, 1, 3), (2, 4), (5,))):
        pick = jnp.zeros((LEVELS, 6 * LEVELS), F32)
        for g in groups:
            pick = pick + jnp.where(j_of == k_of + g * LEVELS, 1.0, 0.0)
        spread = jnp.dot(part, pick.astype(BF16), preferred_element_type=F32)
        total = spread if total is None else total + spread
    weights[...] = total.astype(BF16)
    for pair in straight:
        wait_both_recv(pair)
    coefs(1, HALO + 1)
    coefs(HIGH, ALL - 1)
    outer(rows_of(base.at[3], 0, HALO), rows_of(base.at[3], HIGH, HALO))
    gathered[0, :EDGE] = rows_of(ua, HALO, EDGE)
    gathered[0, EDGE:] = rows_of(ua, HIGH - EDGE, EDGE)
    regroup(gathered, column, 0, all_sem.at[0])
    inner_regions[0].wait_recv()
    blend(1)
    pl.when(middle)(outer_region.wait_recv)
    blend(0)
    regroup(mixed, returned, 0, all_sem.at[1])
    regroup(mixed, returned, 1, all_sem.at[1])

    def take(h, first, start, count):
        o = rows_of(base.at[2], HALO + start, count)
        put_rows(ua, HALO + start, o * returned[h, first : first + count])

    wait_half(returned, 0, all_sem.at[1, 1, 0])
    take(0, 0, 0, EDGE)
    take(0, EDGE, ROWS - EDGE, EDGE)
    sent[0] = ua[SUB * HALO : 2 * SUB * HALO, :]
    sent[1] = ua[SUB * (HIGH - HALO) : SUB * HIGH, :]
    swap = tuple(
        pltpu.make_async_remote_copy(
            src_ref=sent.at[side], dst_ref=got.at[1 - side],
            send_sem=swap_send.at[side], recv_sem=swap_recv.at[side],
            device_id={"tile": tile + 2 * side - 1}, device_id_type=MESH,
        )
        for side in range(2)
    )
    start_both(swap)
    wait_half(returned, 1, all_sem.at[1, 1, 1])
    take(1, 0, EDGE, LEVELS)
    inner()
    wait_both_recv(swap)
    outer(got[0].reshape(HALO, SUB, LANE), got[1].reshape(HALO, SUB, LANE))

    def finish(block, carry):
        r = pl.multiple_of(block * SUB, SUB)
        for c in range(SUB):
            at = (pl.ds(r, SUB), slice(c * LANE, (c + 1) * LANE))
            out_ref[at] = gain[at] * ua[pl.ds((HALO + r) * SUB + c, SUB, stride=SUB), :]
        return carry

    lax.fori_loop(0, ROWS // SUB, finish, 0, unroll=True)

    for ref, sems in ((gathered, all_sem.at[0]), (mixed, all_sem.at[1])):
        for h in range(2):
            part = ref.at[h, pl.ds(0, LEVELS - 1)]
            pltpu.make_async_copy(part, part, sems.at[0, h]).wait()
    for pair in straight:
        wait_both_send(pair)
    wait_both_send(swap)
    inner_regions[0].wait_send()
    pl.when(middle)(inner_regions[1].wait_send)
    for side, carrier in enumerate((down_carrier, up_carrier)):
        pl.when(carrier)(forward(side).wait_send)


def body(*args):
    raw = pltpu.VMEM((ROWS, COLS), F32)
    field = pltpu.VMEM((ALL * SUB, LANE), F32)
    slots = pltpu.VMEM((2, HALO * SUB, LANE), F32)
    cube = pltpu.VMEM((2, LEVELS, SUB, LANE), F32)
    out = pl.pallas_call(
        kernel,
        out_shape=jax.ShapeDtypeStruct((ROWS, COLS), F32),
        in_specs=[pl.BlockSpec(memory_space=pltpu.HBM)] * 7,
        out_specs=pl.BlockSpec(memory_space=pltpu.VMEM),
        scratch_shapes=[
            raw, raw, raw, raw,
            pltpu.VMEM((ROWS, COLS), jnp.int32),
            pltpu.VMEM((1, COLS), jnp.int32),
            pltpu.VMEM((2, 1, COLS), jnp.int32),
            pltpu.VMEM((REGIONS, LEVELS, LEVELS), F32),
            pltpu.VMEM((4, ALL * SUB, LANE), F32),
            field, field, field, field, field, field, field,
            pltpu.VMEM((HALO, 2 * SUB, LANE), F32),
            pltpu.VMEM((HALO, 2 * SUB, LANE), F32),
            slots, slots, slots,
            cube, cube, cube, cube,
            pltpu.VMEM((REGIONS * LEVELS, LEVELS), F32),
            pltpu.VMEM((REGIONS * LEVELS, 6 * LEVELS), BF16),
            pltpu.SemaphoreType.DMA((7,)),
            pltpu.SemaphoreType.DMA((2, 4)),
            pltpu.SemaphoreType.DMA((2, 4)),
            pltpu.SemaphoreType.DMA((2,)),
            pltpu.SemaphoreType.DMA((2,)),
            pltpu.SemaphoreType.DMA((2,)),
            pltpu.SemaphoreType.DMA((2,)),
            pltpu.SemaphoreType.DMA((4,)),
            pltpu.SemaphoreType.DMA((2, 2, 2)),
        ],
        compiler_params=pltpu.CompilerParams(
            collective_id=0, has_side_effects=True, vmem_limit_bytes=32 * 1024 * 1024
        ),
        name="covariance",
    )(*[pltpu.with_memory_space_constraint(x, pltpu.HBM) for x in args])
    return out[None]


def solution(mesh):
    return jax.shard_map(
        body,
        mesh=mesh,
        in_specs=(
            P("lev", "tile", None),
            P("lev", "tile", None),
            P("lev", "tile", None),
            P("lev", "tile", None),
            P("lev", "tile", None),
            P(("tile", "lev"), None),
            P(),
        ),
        out_specs=P("lev", "tile", None),
        check_vma=False,
    )
```

```python
import functools

import jax
import jax.numpy as jnp
from jax import lax
from jax.experimental import pallas as pl
from jax.experimental.pallas import tpu as pltpu
from jax.sharding import PartitionSpec as P

FIELDS = 2
LEVELS = 32
STEPS = 10
REGIONS = 16
ROWS = 64
COLS = 1024
SUB = 8
LANE = 128
EDGE = 16
HALO = 10
HIGH = HALO + ROWS
ALL = HALO + ROWS + HALO
WIDE = 4
BLOCK = 14
MESH = pl.DeviceIdType.MESH
F32 = jnp.float32
BF16 = jnp.bfloat16


def rows_of(ref, start, count):
    return ref[pl.ds(SUB * start, SUB * count), :].reshape(count, SUB, LANE)


def put_rows(ref, start, value):
    count = value.shape[0]
    ref[pl.ds(SUB * start, SUB * count), :] = value.reshape(count * SUB, LANE)


def east_of(x, lane):
    near = pltpu.roll(x, LANE - 1, 2)
    return jnp.where(lane == LANE - 1, pltpu.roll(near, SUB - 1, 1), near)


def west_of(x, lane):
    near = pltpu.roll(x, 1, 2)
    return jnp.where(lane == 0, pltpu.roll(near, 1, 1), near)


def kernel(
    control_hbm, gain_hbm, north_hbm, east_hbm, land_hbm, region_hbm, tiles_hbm,
    out_ref,
    control, gain, north, east, land, own_region, region, tiles,
    base, ua, ub, ca, cn, cs, ce, cw,
    low_past, high_past, carried, sent, got, gathered, column, mixed, returned,
    product, weights,
    in_sem, halo_send, halo_recv, carry_recv, carry_send, swap_send, swap_recv, region_sem, all_sem,
):
    tile = lax.axis_index("tile")
    lev = lax.axis_index("lev")
    tile_count = lax.axis_size("tile")
    which = lev // LEVELS
    mine = lax.rem(lev, LEVELS)
    last = tile_count - 1
    place = lax.rem(tile, WIDE)
    band = tile // WIDE
    bands = tile_count // WIDE
    upper_end = jnp.logical_and(place == WIDE - 1, band < bands - 1)
    lower_end = jnp.logical_and(place == 0, band > 0)
    down_carrier = jnp.logical_and(place > 0, band > 0)
    up_carrier = jnp.logical_and(place < WIDE - 1, band < bands - 1)

    loads = [
        pltpu.make_async_copy(land_hbm.at[0], land, in_sem.at[0]),
        pltpu.make_async_copy(north_hbm.at[0], north, in_sem.at[1]),
        pltpu.make_async_copy(east_hbm.at[0], east, in_sem.at[2]),
        pltpu.make_async_copy(gain_hbm.at[0], gain, in_sem.at[3]),
        pltpu.make_async_copy(control_hbm.at[0], control, in_sem.at[4]),
        pltpu.make_async_copy(region_hbm, own_region, in_sem.at[5]),
        pltpu.make_async_copy(tiles_hbm.at[:, which], tiles, in_sem.at[6]),
    ]
    for load in loads:
        load.start()

    barrier = pltpu.get_barrier_semaphore()

    def group_peer(shift):
        return which * LEVELS + lax.rem(mine + shift, LEVELS)

    @pl.when(tile > 0)
    def _():
        pl.semaphore_signal(barrier, inc=1, device_id={"tile": tile - 1}, device_id_type=MESH)

    @pl.when(tile < last)
    def _():
        pl.semaphore_signal(barrier, inc=1, device_id={"tile": tile + 1}, device_id_type=MESH)

    for far in range(1, WIDE):
        for end, offset in ((upper_end, far + 1), (lower_end, far), (lower_end, -far - 1), (upper_end, -far)):
            @pl.when(end)
            def _(offset=offset):
                pl.semaphore_signal(barrier, inc=1, device_id={"tile": tile + offset}, device_id_type=MESH)

    for carrier, offset in (
        (down_carrier, -place - 1), (down_carrier, -place),
        (up_carrier, WIDE - place), (up_carrier, WIDE - 1 - place),
    ):
        @pl.when(carrier)
        def _(offset=offset):
            pl.semaphore_signal(barrier, inc=1, device_id={"tile": tile + offset}, device_id_type=MESH)

    partner = lax.rem(lev + LEVELS, FIELDS * LEVELS)
    pl.semaphore_signal(barrier, inc=1, device_id={"lev": partner}, device_id_type=MESH)
    middle = jnp.logical_and(lev >= EDGE, lev < ROWS - EDGE)

    @pl.when(middle)
    def _():
        other = lev + EDGE - 2 * EDGE * which
        pl.semaphore_signal(barrier, inc=1, device_id={"lev": other}, device_id_type=MESH)


    def greet(shift, carry):
        pl.semaphore_signal(barrier, inc=1, device_id={"lev": group_peer(shift)}, device_id_type=MESH)
        return carry

    lax.fori_loop(1, LEVELS, greet, 0)

    for load in loads[:5]:
        load.wait()

    def relayout(block, carry):
        r = pl.multiple_of(block * SUB, SUB)
        for c in range(SUB):
            at = (pl.ds(r, SUB), slice(c * LANE, (c + 1) * LANE))
            to = pl.ds((HALO + r) * SUB + c, SUB, stride=SUB)
            ocean = land[at].astype(F32)
            base[0, to, :] = north[at]
            base[1, to, :] = east[at]
            base[2, to, :] = ocean
            start = ocean * gain[at] * control[at]
            base[3, to, :] = start
            ua[to, :] = start
        return carry

    lax.fori_loop(0, ROWS // SUB, relayout, 0, unroll=True)
    loads[5].wait()

    def as_count(flag):
        return flag.astype(jnp.int32)

    greeted = LEVELS + as_count(middle) + as_count(tile > 0) + as_count(tile < last)
    greeted = greeted + 2 * (WIDE - 1) * (as_count(upper_end) + as_count(lower_end))
    greeted = greeted + 2 * (as_count(up_carrier) + as_count(down_carrier))
    pl.semaphore_wait(barrier, greeted)

    def rim(a, start):
        return base.at[a, pl.ds(SUB * start, SUB * HALO), :]

    def send_rim(a, side, offset, to=None):
        start, land_at = ((HALO, HIGH), (HIGH - HALO, 0))[side]
        return pltpu.make_async_remote_copy(
            src_ref=rim(a, start), dst_ref=rim(a, land_at) if to is None else to,
            send_sem=halo_send.at[side, a],
            recv_sem=halo_recv.at[side, a] if to is None else carry_recv.at[side],
            device_id={"tile": tile + offset}, device_id_type=MESH,
        )

    def forward(side):
        a = (place - 1, WIDE - 2 - place)[side]
        return pltpu.make_async_remote_copy(
            src_ref=carried.at[side], dst_ref=rim(a, (HIGH, 0)[side]),
            send_sem=carry_send.at[side], recv_sem=halo_recv.at[side, a],
            device_id={"tile": tile + (-place - 1, WIDE - place)[side]}, device_id_type=MESH,
        )

    has_lower, has_upper = tile > 0, tile < last

    def start_both(pair):
        pl.when(has_lower)(pair[0].start)
        pl.when(has_upper)(pair[1].start)

    def wait_both_recv(pair):
        pl.when(has_upper)(pair[0].wait_recv)
        pl.when(has_lower)(pair[1].wait_recv)

    def wait_both_send(pair):
        pl.when(has_lower)(pair[0].wait_send)
        pl.when(has_upper)(pair[1].wait_send)

    straight = [(send_rim(a, 0, -1), send_rim(a, 1, 1)) for a in range(4)]
    for a in range(WIDE - 1):
        pl.when(lower_end)(send_rim(a, 0, 1 + a, carried.at[0]).start)
        pl.when(upper_end)(send_rim(a, 1, -1 - a, carried.at[1]).start)
    start_both(straight[3])
    for a in range(WIDE - 1):
        pl.when(jnp.logical_and(has_lower, jnp.logical_not(lower_end)))(straight[a][0].start)
        pl.when(jnp.logical_and(has_upper, jnp.logical_not(upper_end)))(straight[a][1].start)

    def carry_on():
        for side, carrier in enumerate((down_carrier, up_carrier)):
            @pl.when(carrier)
            def _(side=side):
                copy = forward(side)
                pltpu.make_async_copy(carried.at[side], carried.at[side], carry_recv.at[side]).wait()
                copy.start()

    def send_region(slot, to, send):
        return pltpu.make_async_remote_copy(
            src_ref=own_region, dst_ref=region.at[slot],
            send_sem=region_sem.at[send], recv_sem=region_sem.at[2 + slot],
            device_id={"lev": to}, device_id_type=MESH,
        )

    outer_region = send_region(0, partner, 0)
    inner_regions = send_region(1, lev - EDGE, 0), send_region(1, lev + EDGE, 1)

    @pl.when(middle)
    def _():
        for copy in inner_regions:
            copy.start()

    @pl.when(jnp.logical_not(middle))
    def _():
        outer_region.start()
        region[0] = own_region[...]

    @pl.when(tile == 0)
    def _():
        for a in range(4):
            base[a, : SUB * HALO, :] = jnp.zeros((SUB * HALO, LANE), F32)
        got[0] = jnp.zeros(got.shape[1:], F32)

    @pl.when(tile == last)
    def _():
        for a in range(4):
            base[a, SUB * HIGH :, :] = jnp.zeros((SUB * HALO, LANE), F32)
        got[1] = jnp.zeros(got.shape[1:], F32)

    first_lane = (1, SUB, LANE)
    lane1 = lax.broadcasted_iota(jnp.int32, first_lane, 2)
    sub1 = lax.broadcasted_iota(jnp.int32, first_lane, 1)
    west_edge = jnp.logical_and(lane1 == 0, sub1 == 0)
    east_edge = jnp.logical_and(lane1 == LANE - 1, sub1 == SUB - 1)

    def make_coef(start, count):
        shape = (count, SUB, LANE)
        lane = jnp.broadcast_to(lane1, shape)
        n = rows_of(base.at[0], start, count)
        s = rows_of(base.at[0], start - 1, count)
        e = rows_of(base.at[1], start, count)
        o = rows_of(base.at[2], start, count)
        w = jnp.where(west_edge, 0.0, west_of(e, lane))
        put_rows(ca, start, o * (1.0 - n - s - e - w))
        put_rows(cn, start, o * n)
        put_rows(cs, start, o * s)
        put_rows(ce, start, o * jnp.where(east_edge, 0.0, e))
        put_rows(cw, start, o * w)

    def coefs(start, end):
        for at in range(start, end, BLOCK):
            make_coef(at, min(BLOCK, end - at))

    def coef_block(b, carry):
        make_coef(HALO + 1 + b * 9, 9)
        return carry

    lax.fori_loop(0, (ROWS - 1) // 9, coef_block, 0)

    def advance(wide, start, count):
        lane = jnp.broadcast_to(lane1, (count, SUB, LANE))
        u = wide[1:-1]
        v = rows_of(ca, start, count) * u
        v = v + rows_of(cn, start, count) * wide[2:]
        v = v + rows_of(cs, start, count) * wide[:-2]
        v = v + rows_of(ce, start, count) * east_of(u, lane)
        return v + rows_of(cw, start, count) * west_of(u, lane)

    def inner_step(src, dst, s):
        low_past[s] = src[pl.ds(SUB * (HALO + s), 2 * SUB), :]
        high_past[s] = src[pl.ds(SUB * (HIGH - 2 - s), 2 * SUB), :]
        at, end = HALO + 1, HIGH - 1
        while at < end:
            count = min(BLOCK, end - at)
            put_rows(dst, at, advance(rows_of(src, at - 1, count + 2), at, count))
            at += count

    def inner():
        def pair(i, carry):
            inner_step(ua, ub, 2 * i)
            inner_step(ub, ua, 2 * i + 1)
            return carry

        lax.fori_loop(0, STEPS // 2, pair, 0)

    def outer(low, high):
        def one(s, carry):
            low, high = carry
            past = low_past[s].reshape(2, SUB, LANE)
            low = advance(jnp.concatenate([low, past], axis=0), 1 + s, HALO)
            past = high_past[s].reshape(2, SUB, LANE)
            high = advance(jnp.concatenate([past, high], axis=0), HIGH - 1 - s, HALO)
            return low, high

        low, high = lax.fori_loop(0, STEPS, one, (low, high))
        put_rows(ua, HALO, low)
        put_rows(ua, HIGH - HALO, high)

    def regroup(src, dst, h, sems):
        def send(shift):
            peer = lax.rem(mine + shift, LEVELS)
            pltpu.make_async_remote_copy(
                src_ref=src.at[h, peer], dst_ref=dst.at[h, mine],
                send_sem=sems.at[0, h], recv_sem=sems.at[1, h],
                device_id={"lev": which * LEVELS + peer}, device_id_type=MESH,
            ).start()

        def six(i, carry):
            for j in range(6):
                send(1 + 6 * i + j)
            return carry

        pltpu.make_async_copy(src.at[h, mine], dst.at[h, mine], sems.at[1, h]).start()
        lax.fori_loop(0, (LEVELS - 1) // 6, six, 0)
        send(LEVELS - 1)

    def wait_half(ref, h, sem):
        pltpu.make_async_copy(ref.at[h], ref.at[h], sem).wait()

    wide = 2 * LANE
    column2 = column.reshape(2 * LEVELS * SUB, LANE)
    mixed2 = mixed.reshape(2 * LEVELS * SUB, LANE)

    def mix(i, carry):
        h = i // (SUB // 2)
        c = 2 * lax.rem(i, SUB // 2)
        start = h * LEVELS * SUB + c
        x = jnp.concatenate(
            [column2[pl.ds(start + q, LEVELS, stride=SUB), :] for q in range(2)], axis=1
        )
        one, two, three = thirds(x)
        stacked = jnp.concatenate([one, two, one, three, two, one], axis=0)
        every = jnp.dot(weights[...], stacked, preferred_element_type=F32)
        ids = region[h, :, pl.ds(pl.multiple_of(c * LANE, wide), wide)]
        ids = jnp.broadcast_to(ids, (LEVELS, wide))
        y = every[:LEVELS]
        for r in range(1, REGIONS):
            y = jnp.where(ids == r, every[r * LEVELS : (r + 1) * LEVELS], y)
        for q in range(2):
            mixed2[pl.ds(start + q, LEVELS, stride=SUB), :] = y[:, q * LANE : (q + 1) * LANE]
        return carry

    def blend(h):
        wait_half(column, h, all_sem.at[0, 1, h])
        lax.fori_loop(h * SUB // 2, (h + 1) * SUB // 2, mix, 0, unroll=True)

    carry_on()
    inner()
    gathered[1] = rows_of(ua, HALO + EDGE, LEVELS)
    regroup(gathered, column, 1, all_sem.at[0])

    loads[6].wait()

    def square(r, carry):
        t = tiles[r]
        m = lax.dot_general(
            t, t, (((0,), (0,)), ((), ())), precision=lax.Precision.HIGHEST, preferred_element_type=F32
        )
        product[pl.ds(pl.multiple_of(r * LEVELS, LEVELS), LEVELS), :] = m
        return carry

    lax.fori_loop(0, REGIONS, square, 0, unroll=True)

    def thirds(x):
        one = x.astype(BF16)
        rest = x - one.astype(F32)
        two = rest.astype(BF16)
        three = (rest - two.astype(F32)).astype(BF16)
        return one, two, three

    k_of = lax.broadcasted_iota(jnp.int32, (LEVELS, 6 * LEVELS), 0)
    j_of = lax.broadcasted_iota(jnp.int32, (LEVELS, 6 * LEVELS), 1)
    total = None
    for part, groups in zip(thirds(product[...]), ((0, 1, 3), (2, 4), (5,))):
        pick = jnp.zeros((LEVELS, 6 * LEVELS), F32)
        for g in groups:
            pick = pick + jnp.where(j_of == k_of + g * LEVELS, 1.0, 0.0)
        spread = jnp.dot(part, pick.astype(BF16), preferred_element_type=F32)
        total = spread if total is None else total + spread
    weights[...] = total.astype(BF16)
    for pair in straight:
        wait_both_recv(pair)
    coefs(1, HALO + 1)
    coefs(HIGH, ALL - 1)
    outer(rows_of(base.at[3], 0, HALO), rows_of(base.at[3], HIGH, HALO))
    gathered[0, :EDGE] = rows_of(ua, HALO, EDGE)
    gathered[0, EDGE:] = rows_of(ua, HIGH - EDGE, EDGE)
    regroup(gathered, column, 0, all_sem.at[0])
    inner_regions[0].wait_recv()
    blend(1)
    pl.when(middle)(outer_region.wait_recv)
    blend(0)
    regroup(mixed, returned, 0, all_sem.at[1])
    regroup(mixed, returned, 1, all_sem.at[1])

    def take(h, first, start, count):
        o = rows_of(base.at[2], HALO + start, count)
        put_rows(ua, HALO + start, o * returned[h, first : first + count])

    wait_half(returned, 0, all_sem.at[1, 1, 0])
    take(0, 0, 0, EDGE)
    take(0, EDGE, ROWS - EDGE, EDGE)
    sent[0] = ua[SUB * HALO : 2 * SUB * HALO, :]
    sent[1] = ua[SUB * (HIGH - HALO) : SUB * HIGH, :]
    swap = tuple(
        pltpu.make_async_remote_copy(
            src_ref=sent.at[side], dst_ref=got.at[1 - side],
            send_sem=swap_send.at[side], recv_sem=swap_recv.at[side],
            device_id={"tile": tile + 2 * side - 1}, device_id_type=MESH,
        )
        for side in range(2)
    )
    start_both(swap)
    wait_half(returned, 1, all_sem.at[1, 1, 1])
    take(1, 0, EDGE, LEVELS)
    inner()
    wait_both_recv(swap)
    outer(got[0].reshape(HALO, SUB, LANE), got[1].reshape(HALO, SUB, LANE))

    def finish(block, carry):
        r = pl.multiple_of(block * SUB, SUB)
        for c in range(SUB):
            at = (pl.ds(r, SUB), slice(c * LANE, (c + 1) * LANE))
            out_ref[at] = gain[at] * ua[pl.ds((HALO + r) * SUB + c, SUB, stride=SUB), :]
        return carry

    lax.fori_loop(0, ROWS // SUB, finish, 0, unroll=True)

    for ref, sems in ((gathered, all_sem.at[0]), (mixed, all_sem.at[1])):
        for h in range(2):
            part = ref.at[h, pl.ds(0, LEVELS - 1)]
            pltpu.make_async_copy(part, part, sems.at[0, h]).wait()
    for pair in straight:
        wait_both_send(pair)
    wait_both_send(swap)
    inner_regions[0].wait_send()
    pl.when(middle)(inner_regions[1].wait_send)
    for side, carrier in enumerate((down_carrier, up_carrier)):
        pl.when(carrier)(forward(side).wait_send)


def body(*args):
    raw = pltpu.VMEM((ROWS, COLS), F32)
    field = pltpu.VMEM((ALL * SUB, LANE), F32)
    slots = pltpu.VMEM((2, HALO * SUB, LANE), F32)
    cube = pltpu.VMEM((2, LEVELS, SUB, LANE), F32)
    out = pl.pallas_call(
        kernel,
        out_shape=jax.ShapeDtypeStruct((ROWS, COLS), F32),
        in_specs=[pl.BlockSpec(memory_space=pltpu.HBM)] * 7,
        out_specs=pl.BlockSpec(memory_space=pltpu.VMEM),
        scratch_shapes=[
            raw, raw, raw, raw,
            pltpu.VMEM((ROWS, COLS), jnp.int32),
            pltpu.VMEM((1, COLS), jnp.int32),
            pltpu.VMEM((2, 1, COLS), jnp.int32),
            pltpu.VMEM((REGIONS, LEVELS, LEVELS), F32),
            pltpu.VMEM((4, ALL * SUB, LANE), F32),
            field, field, field, field, field, field, field,
            pltpu.VMEM((HALO, 2 * SUB, LANE), F32),
            pltpu.VMEM((HALO, 2 * SUB, LANE), F32),
            slots, slots, slots,
            cube, cube, cube, cube,
            pltpu.VMEM((REGIONS * LEVELS, LEVELS), F32),
            pltpu.VMEM((REGIONS * LEVELS, 6 * LEVELS), BF16),
            pltpu.SemaphoreType.DMA((7,)),
            pltpu.SemaphoreType.DMA((2, 4)),
            pltpu.SemaphoreType.DMA((2, 4)),
            pltpu.SemaphoreType.DMA((2,)),
            pltpu.SemaphoreType.DMA((2,)),
            pltpu.SemaphoreType.DMA((2,)),
            pltpu.SemaphoreType.DMA((2,)),
            pltpu.SemaphoreType.DMA((4,)),
            pltpu.SemaphoreType.DMA((2, 2, 2)),
        ],
        compiler_params=pltpu.CompilerParams(
            collective_id=0, has_side_effects=True, vmem_limit_bytes=32 * 1024 * 1024
        ),
        name="covariance",
    )(*[pltpu.with_memory_space_constraint(x, pltpu.HBM) for x in args])
    return out[None]


def solution(mesh):
    return jax.shard_map(
        body,
        mesh=mesh,
        in_specs=(
            P("lev", "tile", None),
            P("lev", "tile", None),
            P("lev", "tile", None),
            P("lev", "tile", None),
            P("lev", "tile", None),
            P(("tile", "lev"), None),
            P(),
        ),
        out_specs=P("lev", "tile", None),
        check_vma=False,
    )
```
